32 devices in a mesh: grp: 8 (over y, x, core), dev: 4 (over z).
Axes of the slice: x: 2, y: 2, z: 4, core: 2. Of those that a mesh axis runs over, the one named last changes fastest.
Arguments:
- tile_patches: bfloat16 [6144, 588], P(('grp', 'dev')), may hold values from -6 to 6
- w_patch: bfloat16 [588, 1536], replicated, may hold values from -0.25 to 0.25
- w_tqkv: bfloat16 [3, 1536, 1536], P(None, None, 'dev'), may hold values from -6 to 6
- w_to: bfloat16 [1536, 1536], P('dev'), may hold values from -0.15625 to 0.15625
- w_gu: bfloat16 [2, 1536, 4096], P(None, None, 'dev'), may hold values from -0.15625 to 0.15625
- w_down: bfloat16 [4096, 1536], P('dev'), may hold values from -0.09375 to 0.09375
- tile_gain: float32 [3, 1536], replicated, may hold values from 0.1 to 1.9
- w_in: bfloat16 [1536, 768], replicated, may hold values from -0.15625 to 0.15625
- slide_tokens: bfloat16 [65536, 768], P(('grp', 'dev')), may hold values from -6 to 6
- slide_gain: float32 [768], replicated, may hold values from 0.1 to 1.9
- w_sqkv: bfloat16 [3, 768, 768], replicated, may hold values from -6 to 6
- w_so: bfloat16 [768, 768], replicated, may hold values from -1.75 to 1.75
- pattern_of_group: int32 [4], replicated, may hold values from 0 to 3, each once
- new_positions: int32 [24], replicated, may hold values from 0 to 65535, as said below
Outputs:
- tile_embed: bfloat16 [24, 768], P('grp')
- slide_out: bfloat16 [65536, 768], P(('grp', 'dev'))
The draws below stay inside these ranges and needn't reach their ends.
Inputs may be any that keep to these rules, and one draw needn't show every extreme that they name: `pattern_of_group`: each of the four patterns is used by exactly one head group. `new_positions`: distinct positions.
All inputs are finite; a program needn't handle non-finite values.
Results may differ from the reference program's by a relative error of at most 0.025.
Values may be sent and summed in bfloat16 or wider, within the bound.
No kernel may reach another device: no remote copies, remote signals or barrier semaphores. Data moves between devices by JAX's collectives and lax.ppermute only.
A program may use at most 256 MiB of HBM per device.

```python
import jax
import jax.numpy as jnp
from jax import lax

TILE_WIDTH = 1536
TILE_HEADS = 24
TILE_HEAD = 64
TILE_HIDDEN = 4096
PATCH_VEC = 588
PATCHES = 256
TILES = 3
SLIDE_WIDTH = 768
SLIDE_HEADS = 16
SLIDE_HEAD = 48
ROWS_DEV = 2048
SEQUENCE = 65536
NEW_TILES = 24
N_GRP = 8
N_DEV = 4


def drawn_heads(seed_key, model_width):
    matrix = jax.random.normal(seed_key, (3, model_width, model_width), jnp.float32) * model_width ** (-0.5)
    return jnp.clip(matrix, -6.0, 6.0)


def draw_w_tqkv(key, part):
    return drawn_heads(jax.random.fold_in(key, 3), TILE_WIDTH).astype(jnp.bfloat16)


def draw_w_sqkv(key, part):
    return drawn_heads(jax.random.fold_in(key, 5), SLIDE_WIDTH).astype(jnp.bfloat16)


def draw_new_positions(key, part):
    return jax.random.permutation(jax.random.fold_in(key, 7), SEQUENCE)[:NEW_TILES].astype(jnp.int32)


def level_of(key, shape, shards, low, high):
    def one(axis_at, blocks):
        heights = jax.random.uniform(jax.random.fold_in(jax.random.fold_in(key, 6), axis_at), (blocks,), jnp.float32, low / len(shards), high / len(shards))
        return jnp.repeat(jnp.exp(heights), shape[axis_at] // blocks).reshape((-1,) + (1,) * (len(shape) - axis_at - 1))

    level = one(*shards[0])
    for cut in shards[1:]:
        level = level * one(*cut)
    return level


def scatter_about(stream_key, shape, scale, limit, split=(), held_as=jnp.bfloat16):
    result = scale * jax.random.normal(stream_key, shape, jnp.float32)
    if split:
        result = result * level_of(stream_key, shape, split, -0.22, 0.18)
    return jnp.clip(result, -limit, limit).astype(held_as)


def setup_inputs(seed: int = 0) -> dict:
    splits = jax.random.split(jax.random.key(seed), 15)
    return {
        "tile_patches": scatter_about(splits[0], (NEW_TILES * PATCHES, PATCH_VEC), 1.0, 6.0, ((0, 32),)),
        "w_patch": scatter_about(splits[1], (PATCH_VEC, TILE_WIDTH), PATCH_VEC ** -0.5, 0.25),
        "w_tqkv": draw_w_tqkv(jax.random.fold_in(splits[14], 71), 0),
        "w_to": scatter_about(splits[3], (TILE_WIDTH, TILE_WIDTH), TILE_WIDTH ** -0.5, 0.15625, ((0, 4),)),
        "w_gu": scatter_about(splits[4], (2, TILE_WIDTH, TILE_HIDDEN), TILE_WIDTH ** -0.5, 0.15625, ((2, 4),)),
        "w_down": scatter_about(splits[5], (TILE_HIDDEN, TILE_WIDTH), TILE_HIDDEN ** -0.5, 0.09375, ((0, 4),)),
        "tile_gain": jnp.clip(1.0 + 0.18 * jax.random.normal(splits[6], (3, TILE_WIDTH), jnp.float32), 0.1, 1.9),
        "w_in": scatter_about(splits[7], (TILE_WIDTH, SLIDE_WIDTH), TILE_WIDTH ** -0.5, 0.15625),
        "slide_tokens": scatter_about(splits[8], (SEQUENCE, SLIDE_WIDTH), 1.0, 6.0, ((0, 32),)),
        "slide_gain": jnp.clip(1.0 + 0.18 * jax.random.normal(splits[9], (SLIDE_WIDTH,), jnp.float32), 0.1, 1.9),
        "w_sqkv": draw_w_sqkv(jax.random.fold_in(splits[14], 71), 0),
        "w_so": scatter_about(splits[11], (SLIDE_WIDTH, SLIDE_WIDTH), (SLIDE_WIDTH // 64) ** -0.5, 1.75),
        "pattern_of_group": jax.random.permutation(splits[12], 4).astype(jnp.int32),
        "new_positions": draw_new_positions(jax.random.fold_in(splits[14], 71), 0),
    }


def layer_norm(inputs, gain):
    inputs = inputs.astype(jnp.float32)
    center = inputs - lax.optimization_barrier(jnp.mean(inputs, axis=-1, keepdims=True))
    spread = lax.optimization_barrier(jnp.mean(center * center, axis=-1, keepdims=True))
    return center * lax.rsqrt(spread + 1e-06) * gain.astype(jnp.float32)

def rounded(inputs):
    return lax.optimization_barrier(inputs.astype(jnp.bfloat16)).astype(jnp.float32)

def block_sum(left, right, blocks):
    row_count = left.shape[0]
    inner = left.shape[1] // blocks
    lower_block_list = left.reshape(row_count, blocks, inner).astype(jnp.float32)
    upper_block_list = right.reshape(blocks, inner, right.shape[1]).astype(jnp.float32)
    running_sums = jnp.einsum('fpa,pam->pfm', lower_block_list, upper_block_list)
    return lax.optimization_barrier(jnp.sum(rounded(running_sums), axis=0))

def attend_tiles(query, keys, values, scale):
    scores = jnp.einsum('bqhd,bkhd->bhqk', query.astype(jnp.float32), keys.astype(jnp.float32)) * scale
    probs = jax.nn.softmax(scores, axis=-1).astype(jnp.bfloat16)
    return jnp.einsum('bhqk,bkhd->bqhd', probs.astype(jnp.float32), values.astype(jnp.float32)).astype(jnp.bfloat16)

def attend_segment(query, keys, values, scale):
    scores = jnp.einsum('qhd,khd->hqk', query.astype(jnp.float32), keys.astype(jnp.float32)) * scale
    probs = jax.nn.softmax(scores, axis=-1).astype(jnp.bfloat16)
    return jnp.einsum('hqk,khd->qhd', probs.astype(jnp.float32), values.astype(jnp.float32)).astype(jnp.bfloat16)

def reference(tile_patches, w_patch, w_tqkv, w_to, w_gu, w_down, tile_gain, w_in, slide_tokens, slide_gain, w_sqkv, w_so, pattern_of_group, new_positions):
    tokens_group = TILES * PATCHES

    def encode_group(patches):
        x_zero = jnp.dot(patches, w_patch, preferred_element_type=jnp.float32).astype(jnp.bfloat16)
        h_one = layer_norm(x_zero, tile_gain[0]).astype(jnp.bfloat16)
        projected = [jnp.dot(h_one, w_tqkv[index], preferred_element_type=jnp.float32).astype(jnp.bfloat16).reshape(TILES, PATCHES, TILE_HEADS, TILE_HEAD) for index in range(3)]
        attended = attend_tiles(projected[0], projected[1], projected[2], TILE_HEAD ** (-0.5)).reshape(tokens_group, TILE_WIDTH)
        x_one = (x_zero.astype(jnp.float32) + block_sum(attended, w_to, N_DEV)).astype(jnp.bfloat16)
        h_two = layer_norm(x_one, tile_gain[1]).astype(jnp.bfloat16)
        gate = jnp.dot(h_two, w_gu[0], preferred_element_type=jnp.float32)
        upward = jnp.dot(h_two, w_gu[1], preferred_element_type=jnp.float32)
        hidden = (jax.nn.silu(gate) * upward).astype(jnp.bfloat16)
        x_two = (x_one.astype(jnp.float32) + block_sum(hidden, w_down, N_DEV)).astype(jnp.bfloat16)
        pooled = lax.optimization_barrier(jnp.mean(x_two.astype(jnp.float32).reshape(TILES, PATCHES, TILE_WIDTH), axis=1))
        normed = layer_norm(pooled, tile_gain[2]).astype(jnp.bfloat16)
        return jnp.dot(normed, w_in, preferred_element_type=jnp.float32).astype(jnp.bfloat16)
    tile_embed = lax.map(encode_group, tile_patches.reshape(N_GRP, tokens_group, PATCH_VEC)).reshape(NEW_TILES, SLIDE_WIDTH)
    seq = slide_tokens.at[new_positions].set(tile_embed)
    h_slide = layer_norm(seq, slide_gain).astype(jnp.bfloat16)
    projected = [jnp.dot(h_slide, w_sqkv[index], preferred_element_type=jnp.float32).astype(jnp.bfloat16) for index in range(3)]
    dilation_rates = (1, N_DEV, N_DEV * N_GRP // 4, N_DEV * N_GRP)
    width_group = SLIDE_WIDTH // 4
    heads_group = SLIDE_HEADS // 4
    attended = jnp.zeros((SEQUENCE, SLIDE_WIDTH), jnp.bfloat16)
    for pattern in range(4):
        ratio = dilation_rates[pattern]
        segments = SEQUENCE // (ratio * ROWS_DEV)
        group = jnp.sum(jnp.where(pattern_of_group == pattern, lax.iota(jnp.int32, 4), 0)).astype(jnp.int32)
        column = (group * width_group).astype(jnp.int32)

        def pick(matrix):
            part = lax.dynamic_slice_in_dim(matrix, column, width_group, 1)
            part = part.reshape(segments, ROWS_DEV, ratio, heads_group, SLIDE_HEAD)
            return jnp.stack([part[:, :, member % ratio, member] for member in range(heads_group)], axis=2)
        picked_entries = [pick(matrix) for matrix in projected]
        outputs = lax.map(lambda triple: attend_segment(triple[0], triple[1], triple[2], SLIDE_HEAD ** (-0.5)), (picked_entries[0], picked_entries[1], picked_entries[2]))
        placed = jnp.zeros((segments, ROWS_DEV, ratio, heads_group, SLIDE_HEAD), jnp.bfloat16)
        for member in range(heads_group):
            placed = placed.at[:, :, member % ratio, member].set(outputs[:, :, member])
        attended = lax.dynamic_update_slice(attended, placed.reshape(SEQUENCE, width_group), (jnp.int32(0), column))
    slide_out = (seq.astype(jnp.float32) + jnp.dot(attended, w_so, preferred_element_type=jnp.float32)).astype(jnp.bfloat16)
    return (tile_embed, slide_out)
```

```python
import functools
import math

import jax
import jax.numpy as jnp
from jax import lax
from jax.experimental import pallas as pl
from jax.experimental.pallas import tpu as pltpu
from jax.sharding import PartitionSpec as P

TILE_HEAD = 64
PATCHES = 256
SLIDE_HEAD = 48
GROUPS = 4
MASKED = -1e30
LOG2E = math.log2(math.e)
F32 = jnp.float32
BF16 = jnp.bfloat16
VMEM_LIMIT = 60 * 1024 * 1024


def norm(x, gain):
    center = x - jnp.mean(x, axis=-1, keepdims=True)
    spread = jnp.mean(center * center, axis=-1, keepdims=True)
    return center * lax.rsqrt(spread + 1e-06) * gain


def mm(a, b):
    return jnp.dot(a, b, preferred_element_type=F32)


def mmt(a, b):
    return lax.dot_general(a, b, (((1,), (1,)), ((), ())), preferred_element_type=F32)


def lanes(shape):
    return lax.broadcasted_iota(jnp.int32, shape, len(shape) - 1)


def params(**kw):
    return pltpu.CompilerParams(vmem_limit_bytes=VMEM_LIMIT, **kw)


def cost(flops, bytes_accessed, trans=0):
    return pl.CostEstimate(flops=int(flops), bytes_accessed=int(bytes_accessed), transcendentals=int(trans))


def whole(shape):
    return pl.BlockSpec(shape, lambda *_: (0,) * len(shape))


def tile_front_kernel(patch_ref, wp_ref, wqkv_ref, gain_ref, x0_ref, att_ref):
    x0 = mm(patch_ref[...], wp_ref[...]).astype(BF16)
    x0_ref[...] = x0
    h1 = norm(x0.astype(F32), gain_ref[0:1, :]).astype(BF16)
    q = (mm(h1, wqkv_ref[0]) * (TILE_HEAD ** -0.5 * LOG2E)).astype(BF16)
    k = mm(h1, wqkv_ref[1]).astype(BF16)
    v = mm(h1, wqkv_ref[2]).astype(BF16)
    width = 2 * TILE_HEAD
    lane = lanes((PATCHES, width))
    for pair in range(q.shape[1] // width):
        cut = slice(pair * width, (pair + 1) * width)
        qp, kp, vp = q[:, cut], k[:, cut], v[:, cut]
        both = []
        for member in range(2):
            here = (lane // TILE_HEAD) == member
            s = mmt(jnp.where(here, qp, jnp.zeros_like(qp)), kp)
            e = jnp.exp2(s - jnp.max(s, axis=1, keepdims=True))
            total = jnp.sum(e, axis=1, keepdims=True)
            both.append(mm(e.astype(BF16), vp) / total)
        att_ref[:, cut] = jnp.where((lane // TILE_HEAD) == 0, both[0], both[1]).astype(BF16)


def tile_front(patches, w_patch, w_tqkv, gain):
    tokens, vec = patches.shape
    width = w_patch.shape[1]
    part = w_tqkv.shape[2]
    return pl.pallas_call(
        tile_front_kernel,
        grid=(tokens // PATCHES,),
        in_specs=[
            pl.BlockSpec((PATCHES, vec), lambda i: (i, 0)),
            whole(w_patch.shape),
            whole(w_tqkv.shape),
            whole(gain.shape),
        ],
        out_specs=[
            pl.BlockSpec((PATCHES, width), lambda i: (i, 0)),
            pl.BlockSpec((PATCHES, part), lambda i: (i, 0)),
        ],
        out_shape=[
            jax.ShapeDtypeStruct((tokens, width), BF16),
            jax.ShapeDtypeStruct((tokens, part), BF16),
        ],
        compiler_params=params(),
        cost_estimate=cost(2 * tokens * width * (vec + 3 * part), 2 * (width * (vec + 3 * part) + tokens * (vec + width + part))),
        name="tile_front",
    )(patches, w_patch, w_tqkv, gain)


def tile_back_kernel(devs, pieces, x0_ref, *rest):
    att_refs = rest[:devs]
    (wto_own, wto_far, wgu_any, wdown_any, gain_ref, order_ref, out_ref, wto, wgu, wdown, hsum, sems) = rest[devs:]
    step = pl.program_id(0)
    rows = wto_own.shape[0]
    piece = rows // pieces

    def far(k, b):
        place = pl.multiple_of(order_ref[b] * piece, piece)
        return pltpu.make_async_copy(wto_far.at[b, k - 1], wto.at[k, pl.ds(place, piece)], sems.at[k])

    def own():
        return pltpu.make_async_copy(wto_own, wto.at[0], sems.at[0])

    def gu(i):
        return pltpu.make_async_copy(wgu_any.at[i], wgu.at[i], sems.at[devs + i])

    def down():
        return pltpu.make_async_copy(wdown_any, wdown, sems.at[devs + 2])

    @pl.when(step == 0)
    def _():
        own().start()
        for k in range(1, devs):
            for b in range(pieces):
                far(k, b).start()
        gu(0).start()
        gu(1).start()
        down().start()
        hsum[...] = jnp.zeros_like(hsum)
        out_ref[...] = jnp.zeros_like(out_ref)
        own().wait()
        for k in range(1, devs):
            for b in range(pieces):
                far(k, b).wait()

    x1 = x0_ref[...].astype(F32)
    for k in range(devs):
        x1 = x1 + mm(att_refs[k][...], wto[k])
    x1 = x1.astype(BF16).astype(F32)
    h2 = norm(x1, gain_ref[1:2, :]).astype(BF16)

    @pl.when(step == 0)
    def _():
        gu(0).wait()
        gu(1).wait()

    gate = mm(h2, wgu[0])
    up = mm(h2, wgu[1])
    hidden = (gate * (1.0 / (1.0 + jnp.exp(-gate))) * up).astype(BF16).astype(F32)
    out_ref[1, pl.ds(step, 1), :] = jnp.mean(x1, axis=0, keepdims=True)
    hsum[pl.ds(step, 1), :] = jnp.mean(hidden, axis=0, keepdims=True)

    @pl.when(step == pl.num_programs(0) - 1)
    def _():
        down().wait()
        high = hsum[...].astype(BF16)
        low = (hsum[...] - high.astype(F32)).astype(BF16)
        out_ref[0] = mm(high, wdown[...]) + mm(low, wdown[...])


def tile_back(x0, atts, wto_own, wto_far, w_gu, w_down, gain, order):
    devs = len(atts)
    pieces = wto_far.shape[0]
    tokens, width = x0.shape
    part = atts[0].shape[1]
    hid = w_gu.shape[2]
    anyspec = pl.BlockSpec(memory_space=pl.ANY)
    return pl.pallas_call(
        functools.partial(tile_back_kernel, devs, pieces),
        grid=(tokens // PATCHES,),
        in_specs=[pl.BlockSpec((PATCHES, width), lambda i: (i, 0))]
        + [pl.BlockSpec((PATCHES, part), lambda i: (i, 0))] * devs
        + [anyspec] * 4
        + [whole(gain.shape), pl.BlockSpec(memory_space=pltpu.SMEM)],
        out_specs=whole((2, 8, width)),
        out_shape=jax.ShapeDtypeStruct((2, 8, width), F32),
        scratch_shapes=[
            pltpu.VMEM((devs, part, width), BF16),
            pltpu.VMEM(w_gu.shape, BF16),
            pltpu.VMEM(w_down.shape, BF16),
            pltpu.VMEM((8, hid), F32),
            pltpu.SemaphoreType.DMA((devs + 3,)),
        ],
        compiler_params=params(),
        cost_estimate=cost(2 * tokens * width * (width + 2 * hid), 2 * width * (width + 3 * hid) + 4 * tokens * width),
        name="tile_back",
    )(x0, *atts, wto_own, wto_far, w_gu, w_down, gain, order)


def embed_kernel(tiles, where_ref, parts_ref, mean_ref, gain_ref, win_ref, out_ref):
    pooled = mean_ref[...]
    for b in range(parts_ref.shape[0]):
        pooled = pooled + parts_ref[where_ref[b]]
    normed = norm(pooled, gain_ref[2:3, :]).astype(BF16)
    out_ref[...] = mm(normed, win_ref[...])[:tiles].astype(BF16)


def embed(where, parts, mean, gain, w_in, tiles):
    return pl.pallas_call(
        functools.partial(embed_kernel, tiles),
        in_specs=[pl.BlockSpec(memory_space=pltpu.SMEM)] + [pl.BlockSpec(memory_space=pltpu.VMEM)] * 4,
        out_specs=pl.BlockSpec(memory_space=pltpu.VMEM),
        out_shape=jax.ShapeDtypeStruct((tiles, w_in.shape[1]), BF16),
        compiler_params=params(),
        cost_estimate=cost(16 * w_in.shape[0] * w_in.shape[1], 2 * w_in.shape[0] * w_in.shape[1]),
        name="tile_embed",
    )(where, parts, mean, gain, w_in)


def head_q(lane):
    return jnp.where(lane < GROUPS * SLIDE_HEAD, lane // SLIDE_HEAD, -1)


def head_sum(lane):
    return jnp.where(lane < 64, lane // 16, (lane - 64) // SLIDE_HEAD)


def stack_heads(q):
    lane = lanes(q.shape)
    owner = head_q(lane)
    flag = GROUPS * SLIDE_HEAD
    parts = []
    for h in range(GROUPS):
        tail = jnp.where(lane == flag + h, 1.0, 0.0).astype(q.dtype)
        parts.append(jnp.where(owner == h, q, tail))
    return jnp.concatenate(parts, axis=0)


def merge_heads(stacked, rows):
    lane = lanes((rows, stacked.shape[1]))
    owner = head_sum(lane)
    out = stacked[0:rows]
    for h in range(1, GROUPS):
        out = jnp.where(owner == h, stacked[h * rows : (h + 1) * rows], out)
    return out


def slide_proj_kernel(ratios, gid_ref, x_ref, gain_ref, w_ref, *rest):
    q_refs = rest[0:4]
    kv0_ref, kvx_ref, held = rest[4:7]
    block = x_ref.shape[0]
    scale = SLIDE_HEAD ** -0.5 * LOG2E
    hs = norm(x_ref[...].astype(F32), gain_ref[...]).astype(BF16)
    wide = hs.astype(F32)
    for c in range(held.shape[0]):
        held[c] = wide[:, c * 128 : (c + 1) * 128]
    y = mm(hs, w_ref[gid_ref[0]])
    q_refs[0][...] = (y[:, :256] * scale).astype(BF16)
    kv0_ref[...] = y[:, 256:].astype(BF16)
    step = pl.program_id(0)
    base = 0
    for p in range(1, 4):
        ratio = ratios[p]
        count = block // ratio
        rows = jnp.concatenate(
            [
                jnp.concatenate(
                    [held[c, pl.ds(j % ratio, count, stride=ratio), :] for j in range(GROUPS)], axis=0
                )
                for c in range(held.shape[0])
            ],
            axis=1,
        ).astype(BF16)
        y = mm(rows, w_ref[gid_ref[p]])
        lane = lanes((count, y.shape[1]))
        flat = jnp.where(lane < 256, lane, lax.rem(lane - 256, GROUPS * SLIDE_HEAD))
        owner = head_q(flat)
        kept = jnp.zeros((count, y.shape[1]), F32)
        for j in range(GROUPS):
            kept = jnp.where(owner == j, y[j * count : (j + 1) * count], kept)
        q_refs[p][...] = (kept[:, :256] * scale).astype(BF16)
        spot = pl.multiple_of(base + step * count, 16)
        kvx_ref[pl.ds(spot, count), :] = kept[:, 256:].astype(BF16)
        base = base + count * pl.num_programs(0)


def slide_block(rows, ratios):
    return min(rows, 16 * ratios[3])


def slide_proj(gid, tokens, gain, w, ratios):
    rows, width = tokens.shape
    block = slide_block(rows, ratios)
    counts = [rows // r for r in ratios]
    return pl.pallas_call(
        functools.partial(slide_proj_kernel, ratios),
        grid_spec=pltpu.PrefetchScalarGridSpec(
            num_scalar_prefetch=1,
            grid=(rows // block,),
            in_specs=[
                pl.BlockSpec((block, width), lambda i, g: (i, 0)),
                whole(gain.shape),
                whole(w.shape),
            ],
            out_specs=[pl.BlockSpec((block // r, 256), lambda i, g: (i, 0)) for r in ratios]
            + [
                pl.BlockSpec((block, 384), lambda i, g: (i, 0)),
                whole((sum(counts[1:]), 384)),
            ],
            scratch_shapes=[pltpu.VMEM((width // 128, block, 128), F32)],
        ),
        out_shape=[jax.ShapeDtypeStruct((c, 256), BF16) for c in counts]
        + [
            jax.ShapeDtypeStruct((rows, 384), BF16),
            jax.ShapeDtypeStruct((sum(counts[1:]), 384), BF16),
        ],
        compiler_params=params(),
        cost_estimate=cost(2 * rows * width * 640 * 2.6, 2 * rows * width * 3 + 2 * w.size),
        name="slide_proj",
    )(gid, tokens, gain, w)


def augment(kv, bias, ka, va):
    keys = kv.shape[0]
    lane = lanes((keys, 256))
    row = lax.broadcasted_iota(jnp.int32, (8, 256), 0)
    spread = jnp.where(lanes((8, 256)) == row + GROUPS * SLIDE_HEAD, 1.0, 0.0).astype(BF16)
    low = lax.dot_general(
        bias.astype(BF16), spread, (((0,), (0,)), ((), ())), preferred_element_type=F32
    ).astype(BF16)
    ka[...] = jnp.where(lane < GROUPS * SLIDE_HEAD, kv[:, 0:256], low)
    va[...] = jnp.where(lane < 64, jnp.ones_like(low), kv[:, 128:384])


def attend(q, ka, va):
    rows = q.shape[0]
    s = mmt(stack_heads(q), ka)
    m = jnp.max(s, axis=1, keepdims=True)
    e = jnp.exp2(s - m).astype(BF16)
    o = mm(e, va)
    sums = merge_heads(o, rows)
    lane = lanes((rows, 128))
    tops = jnp.zeros((rows, 128), F32)
    for h in range(GROUPS):
        tops = jnp.where(lane == h, m[h * rows : (h + 1) * rows], tops)
    return sums, tops


def slide_attend_kernel(q_ref, kv_ref, bias_ref, sum_ref, top_ref, ka, va):
    @pl.when(pl.program_id(0) == 0)
    def _():
        augment(kv_ref, bias_ref[...], ka, va)

    sums, tops = attend(q_ref[...], ka[...], va[...])
    sum_ref[...] = sums
    top_ref[...] = tops


def slide_attend(q, kv, bias, name):
    rows = q.shape[0]
    keys = kv.shape[0]
    block = min(rows, 128)
    return pl.pallas_call(
        slide_attend_kernel,
        grid=(rows // block,),
        in_specs=[
            pl.BlockSpec((block, 256), lambda i: (i, 0)),
            whole(kv.shape),
            whole(bias.shape),
        ],
        out_specs=[
            pl.BlockSpec((block, 256), lambda i: (i, 0)),
            pl.BlockSpec((block, 128), lambda i: (i, 0)),
        ],
        out_shape=[
            jax.ShapeDtypeStruct((rows, 256), F32),
            jax.ShapeDtypeStruct((rows, 128), F32),
        ],
        scratch_shapes=[pltpu.VMEM((keys, 256), BF16), pltpu.VMEM((keys, 256), BF16)],
        compiler_params=params(),
        cost_estimate=cost(4 * 4 * rows * keys * 256, 2 * kv.size + 6 * q.size, 4 * rows * keys),
        name=name,
    )(q, kv, bias)


def fresh_kernel(ratios, news, seg_ref, gid_ref, emb_ref, pos_ref, gain_ref, w_ref, *rest):
    kv_refs = rest[0:4]
    bias_refs = rest[4:8]
    q_ref, sum_ref, top_ref, ka_ref, va_ref, ka, va = rest[8:]
    scale = SLIDE_HEAD ** -0.5 * LOG2E
    hs = norm(emb_ref[...].astype(F32), gain_ref[...]).astype(BF16)
    slots = emb_ref.shape[0]
    pos = pos_ref[...]
    lane = lanes((slots, 256))
    row = lax.broadcasted_iota(jnp.int32, (slots, 256), 0)
    for p in range(4):
        y = mm(hs, w_ref[gid_ref[p]])
        q = (y[:, :256] * scale).astype(BF16)
        kv = y[:, 256:].astype(BF16)
        span = ratios[p] * seg_ref[1]
        same = (pos // span) == (seg_ref[0] // span)
        head = lane - GROUPS * SLIDE_HEAD
        seen = same if ratios[p] == 1 else jnp.logical_and(same, lax.rem(pos, ratios[p]) == head)
        seen = jnp.logical_and(seen, row < news)
        flag = jnp.where(seen, 0.0, MASKED).astype(BF16)
        ka_ref[p] = jnp.where(lane < GROUPS * SLIDE_HEAD, kv[:, 0:256], flag)
        va_ref[p] = jnp.where(lane < 64, jnp.ones_like(flag), kv[:, 128:384])
        q_ref[p] = q.astype(F32)
        augment(kv_refs[p], bias_refs[p][...], ka, va)
        sums, tops = attend(q, ka[...], va[...])
        sum_ref[p] = sums
        top_ref[p] = tops


def fresh(seg, gid, emb, pos, gain, w, kvs, biases, ratios, news):
    slots = emb.shape[0]
    keys = kvs[0].shape[0]
    smem = pl.BlockSpec(memory_space=pltpu.SMEM)
    vmem = pl.BlockSpec(memory_space=pltpu.VMEM)
    return pl.pallas_call(
        functools.partial(fresh_kernel, ratios, news),
        in_specs=[smem, smem] + [vmem] * 12,
        out_specs=[vmem] * 5,
        out_shape=[
            jax.ShapeDtypeStruct((4, slots, 256), F32),
            jax.ShapeDtypeStruct((4, slots, 256), F32),
            jax.ShapeDtypeStruct((4, slots, 128), F32),
            jax.ShapeDtypeStruct((4, slots, 256), BF16),
            jax.ShapeDtypeStruct((4, slots, 256), BF16),
        ],
        scratch_shapes=[pltpu.VMEM((keys, 256), BF16), pltpu.VMEM((keys, 256), BF16)],
        compiler_params=params(),
        cost_estimate=cost(4 * 4 * 4 * slots * keys * 256, 2 * w.size + 8 * kvs[0].size, 16 * slots * keys),
        name="slide_fresh",
    )(seg, gid, emb, pos, gain, w, *kvs, *biases)


def finish_kernel(ratios, news, gid_ref, start_ref, pos_ref, x_ref, emb_ref, wso_ref, *rest):
    q_refs = rest[0:4]
    sum_refs = rest[4:8]
    top_refs = rest[8:12]
    nq_ref, nsum_ref, ntop_ref, nka_ref, nva_ref, out_ref = rest[12:18]
    seq = rest[18]
    qs = rest[19:23]
    ss = rest[23:27]
    ts = rest[27:31]
    placed = rest[31:34]
    step = pl.program_id(0)
    block = x_ref.shape[0]
    start = start_ref[0] + step * block
    seq[...] = x_ref[...].astype(F32)
    for p in range(4):
        qs[p][...] = q_refs[p][...].astype(F32)
        ss[p][...] = sum_refs[p][...]
        ts[p][...] = top_refs[p][...]

    @pl.when(step == 0)
    def _():
        for p in range(1, 4):
            placed[p - 1][...] = jnp.zeros_like(placed[p - 1])

    lane = lanes((1, 256))
    lane_top = lanes((1, 128))

    def patch(n, carry):
        row = pos_ref[n] - start

        @pl.when(jnp.logical_and(row >= 0, row < block))
        def _():
            one = pl.ds(n, 1)
            seq[pl.ds(row, 1), :] = emb_ref[one, :]
            for p in range(4):
                at = pl.ds(row // ratios[p], 1)
                if ratios[p] == 1:
                    qs[p][at, :] = nq_ref[p, one, :]
                    ss[p][at, :] = nsum_ref[p, one, :]
                    ts[p][at, :] = ntop_ref[p, one, :]
                else:
                    head = lax.rem(pos_ref[n], ratios[p])
                    qs[p][at, :] = jnp.where(head_q(lane) == head, nq_ref[p, one, :], qs[p][at, :])
                    ss[p][at, :] = jnp.where(head_sum(lane) == head, nsum_ref[p, one, :], ss[p][at, :])
                    ts[p][at, :] = jnp.where(lane_top == head, ntop_ref[p, one, :], ts[p][at, :])

        return carry

    lax.fori_loop(0, news, patch, 0)

    result = seq[...]
    for p in range(4):
        count = block // ratios[p]
        s = mmt(stack_heads(qs[p][...].astype(BF16)), nka_ref[p])
        tops = ts[p][...]
        old = jnp.concatenate([tops[:, h : h + 1] for h in range(GROUPS)], axis=0)
        top = jnp.maximum(old, jnp.max(s, axis=1, keepdims=True))
        e = jnp.exp2(s - top).astype(BF16)
        shrink = jnp.exp2(old - top)
        o = mm(e, nva_ref[p])
        sums = ss[p][...]
        owner = head_sum(lanes((count, 256)))
        value = jnp.zeros((count, 256), F32)
        for h in range(GROUPS):
            cut = slice(h * count, (h + 1) * count)
            full = sums * shrink[cut] + o[cut]
            weight = full[:, 16 * h : 16 * h + 1]
            value = jnp.where(owner == h, full / weight, value)
        if ratios[p] == 1:
            att = value.astype(BF16)
        else:
            for j in range(GROUPS):
                own = jnp.where(owner == j, value, 0.0)
                for c in range(2):
                    at = pl.ds(j, count, stride=ratios[p])
                    placed[p - 1][c, at, :] = own[:, c * 128 : (c + 1) * 128]
            att = jnp.concatenate([placed[p - 1][0], placed[p - 1][1]], axis=1).astype(BF16)
        result = result + mm(att, wso_ref[gid_ref[p]])
    out_ref[...] = result.astype(BF16)


def finish(gid, start, pos, tokens, emb, wso, qs, sums, tops, new, ratios, news):
    rows, width = tokens.shape
    block = slide_block(rows, ratios)
    counts = [block // r for r in ratios]

    def rowblock(n, lanes_here):
        return pl.BlockSpec((n, lanes_here), lambda i, *_: (i, 0))

    return pl.pallas_call(
        functools.partial(finish_kernel, ratios, news),
        grid_spec=pltpu.PrefetchScalarGridSpec(
            num_scalar_prefetch=3,
            grid=(rows // block,),
            in_specs=[rowblock(block, width), whole(emb.shape), whole(wso.shape)]
            + [rowblock(c, 256) for c in counts]
            + [rowblock(c, 256) for c in counts]
            + [rowblock(c, 128) for c in counts]
            + [whole(a.shape) for a in new],
            out_specs=rowblock(block, width),
            scratch_shapes=[pltpu.VMEM((block, width), F32)]
            + [pltpu.VMEM((c, 256), F32) for c in counts]
            + [pltpu.VMEM((c, 256), F32) for c in counts]
            + [pltpu.VMEM((c, 128), F32) for c in counts]
            + [pltpu.VMEM((2, block, 128), F32)] * 3,
        ),
        out_shape=jax.ShapeDtypeStruct((rows, width), BF16),
        compiler_params=params(),
        cost_estimate=cost(2 * rows * width * 1024, 12 * rows * width),
        name="slide_finish",
    )(gid, start, pos, tokens, emb, wso, *qs, *sums, *tops, *new)


def shifted(x, axis, size, by):
    return lax.ppermute(x, axis, [(i, (i + by) % size) for i in range(size)])


def gather_shifts(x, axis, size):
    return [x] + [shifted(x, axis, size, k) for k in range(1, size)]


def swapped(x, axis, size, bit):
    return lax.ppermute(x, axis, [(i, i ^ bit) for i in range(size)])


def shards(
    tile_patches,
    w_patch,
    w_tqkv,
    w_to,
    w_gu,
    w_down,
    tile_gain,
    w_in,
    slide_tokens,
    slide_gain,
    w_sqkv,
    w_so,
    pattern_of_group,
    new_positions,
):
    devs = lax.axis_size("dev")
    grps = lax.axis_size("grp")
    dev = lax.axis_index("dev")
    grp = lax.axis_index("grp")
    rows, width = slide_tokens.shape
    place = grp * devs + dev
    ratios = (1, devs, devs * grps // 4, devs * grps)
    counts = [rows // r for r in ratios]
    group_width = width // GROUPS
    news = new_positions.shape[0]

    got = gather_shifts(tile_patches, "dev", devs)
    ring = jnp.concatenate(got, axis=0)
    part_rows = tile_patches.shape[0]
    patches = jnp.concatenate(
        [
            lax.dynamic_slice_in_dim(ring, lax.rem(dev - b + devs, devs) * part_rows, part_rows, 0)
            for b in range(devs)
        ],
        axis=0,
    )

    pieces = grps
    while (w_to.shape[0] // pieces) % 16:
        pieces //= 2
    piece_rows = w_to.shape[0] // pieces
    mine = lax.dynamic_slice_in_dim(w_to, lax.rem(grp, pieces) * piece_rows, piece_rows, 0)
    far = jnp.stack(gather_shifts(mine, "dev", devs)[1:])[None]
    bits = [1 << b for b in range(pieces.bit_length() - 1)]
    tags = [0]
    for bit in reversed(bits):
        far = jnp.concatenate([far, swapped(far, "grp", grps, bit)], axis=0)
        tags = tags + [t ^ bit for t in tags]
    order = jnp.bitwise_xor(lax.rem(grp, pieces), jnp.array(tags, jnp.int32))

    gid = jnp.stack(
        [jnp.sum(jnp.where(pattern_of_group == p, lax.iota(jnp.int32, GROUPS), 0)) for p in range(4)]
    ).astype(jnp.int32)
    pieces_w = w_sqkv.reshape(3, width, GROUPS, group_width)
    w_slide = jnp.concatenate(
        [
            jnp.pad(pieces_w[0], ((0, 0), (0, 0), (0, 256 - group_width))),
            pieces_w[1],
            pieces_w[2],
        ],
        axis=-1,
    ).transpose(1, 0, 2)
    w_out = jnp.pad(w_so.reshape(GROUPS, group_width, width), ((0, 0), (256 - group_width, 0), (0, 0)))
    gain_row = slide_gain.reshape(1, width)
    q0, q1, q2, q3, kv0, kvx = slide_proj(gid, slide_tokens, gain_row, w_slide, ratios)
    qs = [q0, q1, q2, q3]

    shipped = gather_shifts(kvx, "dev", devs)
    kv1 = jnp.concatenate([s[: counts[1]] for s in shipped], axis=0)
    tail = jnp.stack([s[counts[1] :] for s in shipped])[None]
    sources = [0]
    near = grps // 4
    for bit in [1 << b for b in range(near.bit_length() - 1)]:
        tail = jnp.concatenate([tail, swapped(tail, "grp", grps, bit)], axis=0)
        sources = sources + [s ^ bit for s in sources]
    near_sources = sources
    kv2 = tail[:, :, : counts[2]].reshape(rows, 384)
    last = tail[:, :, counts[2] :]
    for bit in (near, 2 * near):
        last = jnp.concatenate([last, swapped(last, "grp", grps, bit)], axis=0)
        sources = sources + [s ^ bit for s in sources]
    kv3 = last.reshape(rows, 384)
    kvs = [kv0, kv1, kv2, kv3]

    ring_dev = lax.rem(dev - lax.iota(jnp.int32, devs) + devs, devs)
    blocks = [
        place[None],
        grp * devs + ring_dev,
        (jnp.bitwise_xor(grp, jnp.array(near_sources, jnp.int32))[:, None] * devs + ring_dev[None]).reshape(-1),
        (jnp.bitwise_xor(grp, jnp.array(sources, jnp.int32))[:, None] * devs + ring_dev[None]).reshape(-1),
    ]
    biases = []
    for p in range(4):
        offset = lax.iota(jnp.int32, counts[p]) * ratios[p]
        at = (blocks[p][:, None] * rows + offset[None]).reshape(1, rows)
        head = lax.rem(lax.iota(jnp.int32, 8), ratios[p])[:, None]
        hit = jnp.any((at + head)[:, :, None] == new_positions[None, None, :], axis=-1)
        biases.append(jnp.where(hit, MASKED, 0.0).astype(F32))

    sums, tops = [], []
    for p in range(4):
        s, t = slide_attend(qs[p], kvs[p], biases[p], "slide_attend%d" % p)
        sums.append(s)
        tops.append(t)

    x0, att = tile_front(patches, w_patch, w_tqkv, tile_gain)
    atts = gather_shifts(att, "dev", devs)
    pooled = tile_back(x0, atts, w_to, far, w_gu, w_down, tile_gain, order)
    parts = jnp.stack(gather_shifts(pooled[0], "dev", devs))
    tiles = x0.shape[0] // PATCHES
    tile_embed = embed(ring_dev, parts, pooled[1], tile_gain, w_in, tiles)
    every = lax.all_gather(tile_embed, "grp", axis=0, tiled=True)

    slots = -(-news // 16) * 16
    padded = jnp.pad(every, ((0, slots - news), (0, 0)))
    pos_column = jnp.pad(new_positions, (0, slots - news)).reshape(slots, 1)
    seg = jnp.stack([place * rows, jnp.int32(rows)]).astype(jnp.int32)
    new = fresh(seg, gid, padded, pos_column, gain_row, w_slide, kvs, biases, ratios, news)
    start = (place * rows).reshape(1).astype(jnp.int32)
    slide_out = finish(
        gid, start, new_positions, slide_tokens, padded.astype(F32), w_out, qs, sums, tops, new, ratios, news
    )
    return (tile_embed, slide_out)


def solution(mesh):
    placed = (
        P(("grp", "dev"), None),
        P(),
        P(None, None, "dev"),
        P("dev", None),
        P(None, None, "dev"),
        P("dev", None),
        P(),
        P(),
        P(("grp", "dev"), None),
        P(),
        P(),
        P(),
        P(),
        P(),
    )
    return jax.shard_map(
        shards,
        mesh=mesh,
        in_specs=placed,
        out_specs=(P("grp", None), P(("grp", "dev"), None)),
        check_vma=False,
    )
```

```python
import functools
import math

import jax
import jax.numpy as jnp
from jax import lax
from jax.experimental import pallas as pl
from jax.experimental.pallas import tpu as pltpu
from jax.sharding import PartitionSpec as P


TILE_HEAD = 64
PATCHES = 256
SLIDE_HEAD = 48
GROUPS = 4
MASKED = -1e30
LOG2E = math.log2(math.e)
F32 = jnp.float32
BF16 = jnp.bfloat16
VMEM_LIMIT = 60 * 1024 * 1024


def norm(x, gain):
    center = x - jnp.mean(x, axis=-1, keepdims=True)
    spread = jnp.mean(center * center, axis=-1, keepdims=True)
    return center * lax.rsqrt(spread + 1e-06) * gain


def mm(a, b):
    return jnp.dot(a, b, preferred_element_type=F32)


def mmt(a, b):
    return lax.dot_general(a, b, (((1,), (1,)), ((), ())), preferred_element_type=F32)


def lanes(shape):
    return lax.broadcasted_iota(jnp.int32, shape, len(shape) - 1)


def params(**kw):
    return pltpu.CompilerParams(vmem_limit_bytes=VMEM_LIMIT, **kw)


def cost(flops, bytes_accessed, trans=0):
    return pl.CostEstimate(flops=int(flops), bytes_accessed=int(bytes_accessed), transcendentals=int(trans))


def whole(shape):
    return pl.BlockSpec(shape, lambda *_: (0,) * len(shape))


def tile_front_kernel(devs, where_ref, *rest):
    patch_refs = rest[:devs]
    wp_ref, wqkv_ref, gain_ref, x0_ref, att_ref, held = rest[devs:]
    step = pl.program_id(0)

    @pl.when(step == 0)
    def _():
        count = patch_refs[0].shape[0]
        for k in range(devs):
            held[pl.ds(pl.multiple_of(where_ref[k] * count, count), count), :] = patch_refs[k][...]

    patch = held[pl.ds(pl.multiple_of(step * PATCHES, PATCHES), PATCHES), :]
    x0 = mm(patch, wp_ref[...]).astype(BF16)
    x0_ref[...] = x0
    h1 = norm(x0.astype(F32), gain_ref[0:1, :]).astype(BF16)
    q = (mm(h1, wqkv_ref[0]) * (TILE_HEAD ** -0.5 * LOG2E)).astype(BF16)
    k = mm(h1, wqkv_ref[1]).astype(BF16)
    v = mm(h1, wqkv_ref[2]).astype(BF16)
    width = 2 * TILE_HEAD
    first = lanes((PATCHES, width)) < TILE_HEAD
    for pair in range(q.shape[1] // width):
        cut = slice(pair * width, (pair + 1) * width)
        qp, kp, vp = q[:, cut], k[:, cut], v[:, cut]
        none = jnp.zeros_like(qp)
        both = []
        for s in (mmt(jnp.where(first, qp, none), kp), mmt(jnp.where(first, none, qp), kp)):
            e = jnp.exp2(s - jnp.max(s, axis=1, keepdims=True))
            total = jnp.sum(e, axis=1, keepdims=True)
            both.append(mm(e.astype(BF16), vp) / total)
        att_ref[:, cut] = jnp.where(first, both[0], both[1]).astype(BF16)


def tile_front(where, patches, w_patch, w_tqkv, gain):
    devs = len(patches)
    count, vec = patches[0].shape
    tokens = devs * count
    width = w_patch.shape[1]
    part = w_tqkv.shape[2]
    return pl.pallas_call(
        functools.partial(tile_front_kernel, devs),
        grid=(tokens // PATCHES,),
        in_specs=[pl.BlockSpec(memory_space=pltpu.SMEM)]
        + [whole((count, vec))] * devs
        + [
            whole(w_patch.shape),
            whole(w_tqkv.shape),
            whole(gain.shape),
        ],
        out_specs=[
            pl.BlockSpec((PATCHES, width), lambda i: (i, 0)),
            pl.BlockSpec((PATCHES, part), lambda i: (i, 0)),
        ],
        out_shape=[
            jax.ShapeDtypeStruct((tokens, width), BF16),
            jax.ShapeDtypeStruct((tokens, part), BF16),
        ],
        scratch_shapes=[pltpu.VMEM((tokens, vec), BF16)],
        compiler_params=params(),
        cost_estimate=cost(2 * tokens * width * (vec + 3 * part), 2 * (width * (vec + 3 * part) + tokens * (vec + width + part))),
        name="tile_front",
    )(where, *patches, w_patch, w_tqkv, gain)


def tile_back_kernel(devs, pieces, x0_ref, *rest):
    att_refs = rest[: 2 * devs - 1]
    rest = rest[2 * devs - 1 :]
    far_refs = rest[:pieces]
    (wto_own, wgu_any, wdown_any, gain_ref, order_ref, out_ref, wto, wgu, wdown, hsum, sems) = rest[pieces:]
    step = pl.program_id(0)
    rows = wto_own.shape[0]
    piece = rows // pieces

    def far(k, b):
        place = pl.multiple_of(order_ref[b] * piece, piece)
        return pltpu.make_async_copy(far_refs[b].at[k, pl.ds(0, piece)], wto.at[k, pl.ds(place, piece)], sems.at[k])

    def own():
        return pltpu.make_async_copy(wto_own, wto.at[0], sems.at[0])

    def gu(i):
        return pltpu.make_async_copy(wgu_any.at[i], wgu.at[i], sems.at[devs + i])

    def down():
        return pltpu.make_async_copy(wdown_any, wdown, sems.at[devs + 2])

    @pl.when(step == 0)
    def _():
        own().start()
        for k in range(1, devs):
            for b in range(pieces):
                far(k, b).start()
        gu(0).start()
        gu(1).start()
        down().start()
        hsum[...] = jnp.zeros_like(hsum)
        out_ref[...] = jnp.zeros_like(out_ref)
        own().wait()
        for k in range(1, devs):
            for b in range(pieces):
                far(k, b).wait()

    x1 = x0_ref[...].astype(F32) + mm(att_refs[0][...], wto[0])
    for k in range(1, devs):
        near = order_ref[pieces] >= k
        att = jnp.where(near, att_refs[2 * k - 1][...], att_refs[2 * k][...])
        x1 = x1 + mm(att, wto[k])
    x1 = x1.astype(BF16).astype(F32)
    h2 = norm(x1, gain_ref[1:2, :]).astype(BF16)

    @pl.when(step == 0)
    def _():
        gu(0).wait()
        gu(1).wait()

    gate = mm(h2, wgu[0])
    up = mm(h2, wgu[1])
    hidden = (gate * (1.0 / (1.0 + jnp.exp(-gate))) * up).astype(BF16).astype(F32)
    out_ref[1, pl.ds(step, 1), :] = jnp.mean(x1, axis=0, keepdims=True)
    hsum[pl.ds(step, 1), :] = jnp.mean(hidden, axis=0, keepdims=True)

    @pl.when(step == pl.num_programs(0) - 1)
    def _():
        down().wait()
        high = hsum[...].astype(BF16)
        low = (hsum[...] - high.astype(F32)).astype(BF16)
        out_ref[0] = mm(high, wdown[...]) + mm(low, wdown[...])


def tile_back(x0, atts, wto_own, wto_far, w_gu, w_down, gain, order):
    devs = len(atts)
    atts = atts[:1] + [a for pair in atts[1:] for a in pair]
    pieces = len(wto_far)
    tokens, width = x0.shape
    part = atts[0].shape[1]
    hid = w_gu.shape[2]
    anyspec = pl.BlockSpec(memory_space=pl.ANY)
    return pl.pallas_call(
        functools.partial(tile_back_kernel, devs, pieces),
        grid=(tokens // PATCHES,),
        in_specs=[pl.BlockSpec((PATCHES, width), lambda i: (i, 0))]
        + [pl.BlockSpec((PATCHES, part), lambda i: (i, 0))] * (2 * devs - 1)
        + [anyspec] * (pieces + 3)
        + [whole(gain.shape), pl.BlockSpec(memory_space=pltpu.SMEM)],
        out_specs=whole((2, 8, width)),
        out_shape=jax.ShapeDtypeStruct((2, 8, width), F32),
        scratch_shapes=[
            pltpu.VMEM((devs, part, width), BF16),
            pltpu.VMEM(w_gu.shape, BF16),
            pltpu.VMEM(w_down.shape, BF16),
            pltpu.VMEM((8, hid), F32),
            pltpu.SemaphoreType.DMA((devs + 3,)),
        ],
        compiler_params=params(),
        cost_estimate=cost(2 * tokens * width * (width + 2 * hid), 2 * width * (width + 3 * hid) + 4 * tokens * width),
        name="tile_back",
    )(x0, *atts, *wto_far, wto_own, w_gu, w_down, gain, order)


def embed_kernel(tiles, where_ref, parts_ref, mean_ref, gain_ref, win_ref, out_ref):
    pooled = mean_ref[...]
    for b in range(parts_ref.shape[0]):
        pooled = pooled + parts_ref[where_ref[b]]
    normed = norm(pooled, gain_ref[2:3, :]).astype(BF16)
    out_ref[...] = mm(normed, win_ref[...])[:tiles].astype(BF16)


def embed(where, parts, mean, gain, w_in, tiles):
    return pl.pallas_call(
        functools.partial(embed_kernel, tiles),
        in_specs=[pl.BlockSpec(memory_space=pltpu.SMEM)] + [pl.BlockSpec(memory_space=pltpu.VMEM)] * 4,
        out_specs=pl.BlockSpec(memory_space=pltpu.VMEM),
        out_shape=jax.ShapeDtypeStruct((tiles, w_in.shape[1]), BF16),
        compiler_params=params(),
        cost_estimate=cost(16 * w_in.shape[0] * w_in.shape[1], 2 * w_in.shape[0] * w_in.shape[1]),
        name="tile_embed",
    )(where, parts, mean, gain, w_in)


USED = GROUPS * SLIDE_HEAD
FLAGS = 256 - USED
SHARE = FLAGS // GROUPS


def between(lane, low, count):
    return jnp.logical_and(lane >= low, lane < low + count)


def own_q(lane, h):
    return between(lane, FLAGS + SLIDE_HEAD * h, SLIDE_HEAD)


def own_sum(lane, h):
    return jnp.logical_or(between(lane, SLIDE_HEAD * h, SLIDE_HEAD), between(lane, USED + SHARE * h, SHARE))


def flagged(q):
    return jnp.where(lanes(q.shape) < GROUPS, 1.0, q).astype(BF16)


def one_head(q, lane, h):
    return jnp.where(own_q(lane, h), q, jnp.where(lane == h, 1.0, 0.0).astype(q.dtype))


def slide_proj_kernel(ratios, gid_ref, x_ref, gain_ref, w_any, *rest):
    q_refs = rest[0:4]
    kv0_ref, near_ref, far_ref, w_ref, held = rest[4:9]
    block, width = x_ref.shape
    scale = SLIDE_HEAD ** -0.5 * LOG2E
    step = pl.program_id(0)

    @pl.when(step == 0)
    def _():
        w_ref[:, :, 0:FLAGS] = jnp.zeros((GROUPS, width, FLAGS), BF16)
        for g in range(GROUPS):
            cut = slice(g * USED, (g + 1) * USED)
            w_ref[g, :, FLAGS:256] = w_any[0, :, cut]
            w_ref[g, :, 256 : 256 + USED] = w_any[2, :, cut]
            w_ref[g, :, 256 + USED : 256 + 2 * USED] = w_any[1, :, cut]

    hs = norm(x_ref[...].astype(F32), gain_ref[...]).astype(BF16)
    wide = hs.astype(F32)
    for c in range(held.shape[0]):
        held[c] = wide[:, c * 128 : (c + 1) * 128]
    y = mm(hs, w_ref[gid_ref[0]])
    q_refs[0][...] = flagged(y[:, :256] * scale)
    kv0_ref[...] = y[:, 256:].astype(BF16)
    base = 0
    for p in range(1, 4):
        ratio = ratios[p]
        count = block // ratio
        rows = jnp.concatenate(
            [
                jnp.concatenate(
                    [held[c, pl.ds(j % ratio, count, stride=ratio), :] for j in range(GROUPS)], axis=0
                )
                for c in range(held.shape[0])
            ],
            axis=1,
        ).astype(BF16)
        y = mm(rows, w_ref[gid_ref[p]])
        lane = lanes((count, y.shape[1])) - FLAGS
        kept = y[0:count]
        for j in range(1, GROUPS):
            here = between(lane, SLIDE_HEAD * j, SLIDE_HEAD)
            here = jnp.logical_or(here, between(lane, USED + SLIDE_HEAD * j, SLIDE_HEAD))
            here = jnp.logical_or(here, between(lane, 2 * USED + SLIDE_HEAD * j, SLIDE_HEAD))
            kept = jnp.where(here, y[j * count : (j + 1) * count], kept)
        q_refs[p][...] = flagged(kept[:, :256] * scale)
        if p == 3:
            far_ref[...] = kept[:, 256:].astype(BF16)
        else:
            spot = pl.multiple_of(base + step * count, 16)
            near_ref[pl.ds(spot, count), :] = kept[:, 256:].astype(BF16)
            base = base + count * pl.num_programs(0)


def slide_block(rows, ratios):
    return min(rows, 16 * ratios[3])


def slide_proj(gid, tokens, gain, w, ratios):
    rows, width = tokens.shape
    block = slide_block(rows, ratios)
    counts = [rows // r for r in ratios]
    wide = (GROUPS, width, 256 + 2 * USED)
    return pl.pallas_call(
        functools.partial(slide_proj_kernel, ratios),
        grid_spec=pltpu.PrefetchScalarGridSpec(
            num_scalar_prefetch=1,
            grid=(rows // block,),
            in_specs=[
                pl.BlockSpec((block, width), lambda i, g: (i, 0)),
                whole(gain.shape),
                whole(w.shape),
            ],
            out_specs=[pl.BlockSpec((block // r, 256), lambda i, g: (i, 0)) for r in ratios]
            + [
                pl.BlockSpec((block, 2 * USED), lambda i, g: (i, 0)),
                whole((sum(counts[1:3]), 2 * USED)),
                pl.BlockSpec((block // ratios[3], 2 * USED), lambda i, g: (0, i)),
                whole(wide),
            ],
            scratch_shapes=[pltpu.VMEM((width // 128, block, 128), F32)],
        ),
        out_shape=[jax.ShapeDtypeStruct((c, 256), BF16) for c in counts]
        + [
            jax.ShapeDtypeStruct((rows, 2 * USED), BF16),
            jax.ShapeDtypeStruct((sum(counts[1:3]), 2 * USED), BF16),
            jax.ShapeDtypeStruct((block // ratios[3], rows // block * 2 * USED), BF16),
            jax.ShapeDtypeStruct(wide, BF16),
        ],
        compiler_params=params(),
        cost_estimate=cost(2 * rows * width * 640 * 2.6, 2 * rows * width * 3 + 2 * w.size),
        name="slide_proj",
    )(gid, tokens, gain, w)


def augment(pieces, at, ratio, pos_ref, news, ka, va):
    keys = ka.shape[0]
    head = lax.broadcasted_iota(jnp.int32, (8, keys), 0)
    here = jnp.broadcast_to(at, (8, keys))
    if ratio > 1:
        here = here + head
    low = jnp.zeros((8, keys), F32)
    for n in range(news):
        low = jnp.where(here == pos_ref[n], MASKED, low)
    spread = jnp.where(lanes((8, 256)) == lax.broadcasted_iota(jnp.int32, (8, 256), 0), 1.0, 0.0).astype(BF16)
    low = lax.dot_general(
        low.astype(BF16), spread, (((0,), (0,)), ((), ())), preferred_element_type=F32
    ).astype(BF16)
    spot = 0
    for load in pieces:
        value, key = load()
        count = value.shape[0]
        lane = lanes((count, 256))
        cut = slice(spot, spot + count)
        ka[cut] = jnp.where(lane < FLAGS, low[cut], key)
        va[cut] = jnp.where(lane < USED, value, jnp.ones_like(value))
        spot += count


def state(sums, tops):
    rows = sums.shape[0]
    low = sums[:, 128:256]
    lane = lanes((rows, 128))
    for h in range(GROUPS):
        low = jnp.where(between(lane, USED - 128 + SHARE * h + 8, 8), tops[h], low)
    return jnp.transpose(low)[USED - 128 :]


def attend(q, ka, va):
    rows = q.shape[0]
    lane = lanes(q.shape)
    tops = []
    sums = jnp.zeros((rows, 256), F32)
    s = mmt(one_head(q, lane, 0), ka[...])
    for h in range(GROUPS):
        after = mmt(one_head(q, lane, h + 1), ka[...]) if h + 1 < GROUPS else None
        m = jnp.max(s, axis=1, keepdims=True)
        o = mm(jnp.exp2(s - m).astype(BF16), va[...])
        sums = jnp.where(own_sum(lane, h), o, sums)
        tops.append(m)
        s = after
    return sums, state(sums, tops)


def attend_stacked(q, ka, va):
    rows = q.shape[0]
    lane = lanes(q.shape)
    s = mmt(jnp.concatenate([one_head(q, lane, h) for h in range(GROUPS)], axis=0), ka[...])
    m = jnp.max(s, axis=1, keepdims=True)
    o = mm(jnp.exp2(s - m).astype(BF16), va[...])
    sums = o[0:rows]
    for h in range(1, GROUPS):
        sums = jnp.where(own_sum(lane, h), o[h * rows : (h + 1) * rows], sums)
    return sums, state(sums, [m[h * rows : (h + 1) * rows] for h in range(GROUPS)])


def loaders(refs, cuts):
    made = []
    for ref, cut in zip(refs, cuts):

        def load(ref=ref, cut=cut):
            index = cut[:-2] + (slice(cut[-2][0], cut[-2][1]),)
            lane = cut[-1]
            return ref[index + (slice(lane, lane + 256),)], ref[index + (slice(lane + 128, lane + 384),)]

        made.append(load)
    return made


def slide_attend_kernel(ratio, news, cuts, used, pos_ref, at_ref, q_ref, *rest):
    count = max(used) + 1
    kv_refs = rest[:count]
    sum_ref, top_ref, ka, va = rest[-4:]

    @pl.when(pl.program_id(0) == 0)
    def _():
        augment(loaders([kv_refs[u] for u in used], cuts), at_ref[...], ratio, pos_ref, news, ka, va)

    small = q_ref.shape[0] < 128
    sums, tops = (attend_stacked if small else attend)(q_ref[...], ka, va)
    sum_ref[...] = sums
    if len(top_ref.shape) == 2:
        top_ref[...] = tops
    else:
        size = top_ref.shape[2]
        for u in range(top_ref.shape[0]):
            top_ref[u] = tops[:, u * size : (u + 1) * size]


def slide_attend(pos, at, q, kv, ratio, size, half=None, earlier=()):
    arrays, used, cuts = kv
    rows = q.shape[0]
    keys = at.shape[1]
    block = min(rows, 256)
    steps = rows // block
    first = 0
    if half is not None:
        first, steps = half * (steps // 2), steps // 2
    smem = pl.BlockSpec(memory_space=pltpu.SMEM)
    if block <= size:
        per = size // block
        top_spec = pl.BlockSpec((None, FLAGS, block), lambda i: ((i + first) // per, 0, (i + first) % per))
    else:
        top_spec = pl.BlockSpec((block // size, FLAGS, size), lambda i: (i + first, 0, 0))
    done = steps * block
    return pl.pallas_call(
        functools.partial(slide_attend_kernel, ratio, pos.shape[0], cuts, used),
        grid=(steps,),
        in_specs=[
            smem,
            whole(at.shape),
            pl.BlockSpec((block, 256), lambda i: (i + first, 0)),
        ]
        + [whole(a.shape) for a in arrays]
        + [pl.BlockSpec(memory_space=pl.ANY)] * len(earlier),
        out_specs=[
            pl.BlockSpec((block, 256), lambda i: (i + first, 0)),
            top_spec,
        ],
        out_shape=[
            jax.ShapeDtypeStruct((rows, 256), F32),
            jax.ShapeDtypeStruct((rows // size, FLAGS, size), F32),
        ],
        scratch_shapes=[pltpu.VMEM((keys, 256), BF16), pltpu.VMEM((keys, 256), BF16)],
        input_output_aliases={3 + len(arrays) + i: i for i in range(len(earlier))},
        compiler_params=params(),
        cost_estimate=cost(4 * 4 * done * keys * 256, 2 * keys * 384 + 6 * done * 256, 4 * done * keys),
    )(pos, at, q, *arrays, *earlier)


def fresh_kernel(ratios, news, plan, seg_ref, gid_ref, news_ref, emb_ref, pos_ref, gain_ref, w_ref, at_ref, *rest):
    total = sum(n for n, _, _ in plan)
    kv_refs = rest[:total]
    q_ref, sum_ref, top_ref, ka_ref, va_ref, ka, va = rest[total:]
    scale = SLIDE_HEAD ** -0.5 * LOG2E
    hs = norm(emb_ref[...], gain_ref[...]).astype(BF16)
    slots = emb_ref.shape[0]
    pos = pos_ref[...]
    lane = lanes((slots, 256))
    row = lax.broadcasted_iota(jnp.int32, (slots, 256), 0)
    first = 0
    for p in range(4):
        y = mm(hs, w_ref[gid_ref[p]])
        q = flagged(y[:, :256] * scale)
        kv = y[:, 256:].astype(BF16)
        span = ratios[p] * seg_ref[1]
        same = (pos // span) == (seg_ref[0] // span)
        seen = jnp.broadcast_to(same, lane.shape)
        if ratios[p] > 1:
            seen = jnp.logical_and(seen, lax.rem(pos, ratios[p]) == lane)
        seen = jnp.logical_and(seen, row < news)
        flag = jnp.where(seen, 0.0, MASKED).astype(BF16)
        none = jnp.zeros_like(flag)
        for h in range(GROUPS):
            key = jnp.where(own_q(lane, h), kv[:, 128:384], jnp.where(lane == h, flag, none))
            ka_ref[p, h * slots : (h + 1) * slots] = key
            va_ref[p, h * slots : (h + 1) * slots] = jnp.where(between(lane, SLIDE_HEAD * h, SLIDE_HEAD), kv[:, 0:256], none)
        q_ref[p] = q.astype(F32)
        count, used, cuts = plan[p]
        refs = kv_refs[first : first + count]
        first += count
        augment(loaders([refs[u] for u in used], cuts), at_ref[p], ratios[p], news_ref, news, ka, va)
        sums, tops = attend_stacked(q, ka, va)
        sum_ref[p] = sums
        top_ref[p] = tops


def fresh(seg, gid, news_pos, emb, pos, gain, w, at, kvs, ratios):
    slots = emb.shape[0]
    keys = at.shape[-1]
    smem = pl.BlockSpec(memory_space=pltpu.SMEM)
    vmem = pl.BlockSpec(memory_space=pltpu.VMEM)
    plan = [(len(arrays), used, cuts) for arrays, used, cuts in kvs]
    flat = [a for arrays, _, _ in kvs for a in arrays]
    return pl.pallas_call(
        functools.partial(fresh_kernel, ratios, news_pos.shape[0], plan),
        in_specs=[smem] * 3 + [vmem] * (5 + len(flat)),
        out_specs=[vmem] * 5,
        out_shape=[
            jax.ShapeDtypeStruct((4, slots, 256), F32),
            jax.ShapeDtypeStruct((4, slots, 256), F32),
            jax.ShapeDtypeStruct((4, FLAGS, slots), F32),
            jax.ShapeDtypeStruct((4, GROUPS * slots, 256), BF16),
            jax.ShapeDtypeStruct((4, GROUPS * slots, 256), BF16),
        ],
        scratch_shapes=[pltpu.VMEM((keys, 256), BF16), pltpu.VMEM((keys, 256), BF16)],
        compiler_params=params(),
        cost_estimate=cost(4 * 4 * 4 * slots * keys * 256, 2 * w.size + 8 * keys * 384, 16 * slots * keys),
        name="slide_fresh",
    )(seg, gid, news_pos, emb, pos, gain, w, at, *flat)


def finish_kernel(ratios, news, gid_ref, start_ref, pos_ref, x_ref, emb_ref, wso_ref, *rest):
    q_refs = rest[0:4]
    sum_refs = rest[4:8]
    top_refs = rest[8:12]
    nq_ref, nsum_ref, ntop_ref, nka_ref, nva_ref, out_ref = rest[12:18]
    seq = rest[18]
    qs = rest[19:23]
    ss = rest[23:27]
    ts = rest[27:31]
    placed = rest[31:34]
    step = pl.program_id(0)
    block = x_ref.shape[0]
    start = start_ref[0] + step * block
    seq[...] = x_ref[...].astype(F32)
    for p in range(4):
        qs[p][...] = q_refs[p][...].astype(F32)
        ss[p][...] = sum_refs[p][...]
        ts[p][...] = top_refs[p][...]

    @pl.when(step == 0)
    def _():
        for p in range(1, 4):
            placed[p - 1][...] = jnp.zeros_like(placed[p - 1])

    lane = lanes((1, 256))

    def patch(n, carry):
        row = pos_ref[n] - start

        @pl.when(jnp.logical_and(row >= 0, row < block))
        def _():
            one = pl.ds(n, 1)
            seq[pl.ds(row, 1), :] = emb_ref[one, :]
            for p in range(4):
                spot = row // ratios[p]
                at = pl.ds(spot, 1)
                fresh_state = ntop_ref[p]
                column = jnp.sum(jnp.where(lanes(fresh_state.shape) == n, fresh_state, 0.0), axis=1, keepdims=True)
                held_state = ts[p][...]
                mine = lanes(held_state.shape) == spot
                if ratios[p] == 1:
                    qs[p][at, :] = nq_ref[p, one, :]
                    ss[p][at, :] = nsum_ref[p, one, :]
                else:
                    head = lax.rem(pos_ref[n], ratios[p])
                    fits = head < GROUPS
                    mine_q = jnp.logical_and(own_q(lane, head), fits)
                    mine_sum = jnp.logical_and(own_sum(lane, head), fits)
                    qs[p][at, :] = jnp.where(mine_q, nq_ref[p, one, :], qs[p][at, :])
                    ss[p][at, :] = jnp.where(mine_sum, nsum_ref[p, one, :], ss[p][at, :])
                    line = lax.broadcasted_iota(jnp.int32, held_state.shape, 0)
                    mine = jnp.logical_and(mine, between(line, SHARE * head, SHARE))
                ts[p][...] = jnp.where(mine, column, held_state)

        return carry

    lax.fori_loop(0, news, patch, 0)

    slots = nka_ref.shape[1] // GROUPS
    owner = lanes((24, 256)) // SLIDE_HEAD
    spread = jnp.where(owner == lax.rem(lax.broadcasted_iota(jnp.int32, (24, 256), 0), 8), 1.0, 0.0).astype(BF16)
    result = seq[...]
    for p in range(4):
        count = block // ratios[p]
        s = mmt(nka_ref[p], qs[p][...].astype(BF16))
        weights = []
        scale = jnp.zeros((8, count), F32)
        line = lax.broadcasted_iota(jnp.int32, (8, count), 0)
        for h in range(GROUPS):
            own = s[h * slots : (h + 1) * slots]
            total = ts[p][SHARE * h : SHARE * h + 1]
            old = ts[p][SHARE * h + 8 : SHARE * h + 9]
            top = jnp.maximum(old, jnp.max(own, axis=0, keepdims=True))
            e = jnp.exp2(own - top)
            shrink = jnp.exp2(old - top)
            inverse = 1.0 / (total * shrink + jnp.sum(e, axis=0, keepdims=True))
            weights.append((e * inverse).astype(BF16))
            scale = jnp.where(line == h, shrink * inverse, scale)
        o = lax.dot_general(
            jnp.concatenate(weights, axis=0), nva_ref[p], (((0,), (0,)), ((), ())), preferred_element_type=F32
        )
        high = scale.astype(BF16)
        rest_one = scale - high.astype(F32)
        middle = rest_one.astype(BF16)
        low = (rest_one - middle.astype(F32)).astype(BF16)
        split = jnp.concatenate([high.astype(F32), middle.astype(F32), low.astype(F32)], axis=0).astype(BF16)
        wide = lax.dot_general(split, spread, (((0,), (0,)), ((), ())), preferred_element_type=F32)
        value = ss[p][...] * wide + o
        if ratios[p] == 1:
            att = value[:, :USED].astype(BF16)
        else:
            lane_wide = lanes((count, 256))
            for j in range(GROUPS):
                own = jnp.where(between(lane_wide, SLIDE_HEAD * j, SLIDE_HEAD), value, 0.0)
                for c in range(2):
                    at = pl.ds(j, count, stride=ratios[p])
                    placed[p - 1][c, at, :] = own[:, c * 128 : (c + 1) * 128]
            att = jnp.concatenate([placed[p - 1][0], placed[p - 1][1]], axis=1)[:, :USED].astype(BF16)
        result = result + mm(att, wso_ref[gid_ref[p]])
    out_ref[...] = result.astype(BF16)


def finish(gid, start, pos, tokens, emb, wso, qs, sums, tops, new, ratios, news):
    rows, width = tokens.shape
    block = slide_block(rows, ratios)
    counts = [block // r for r in ratios]

    def rowblock(n, lanes_here):
        return pl.BlockSpec((n, lanes_here), lambda i, *_: (i, 0))

    return pl.pallas_call(
        functools.partial(finish_kernel, ratios, news),
        grid_spec=pltpu.PrefetchScalarGridSpec(
            num_scalar_prefetch=3,
            grid=(rows // block,),
            in_specs=[rowblock(block, width), whole(emb.shape), whole(wso.shape)]
            + [rowblock(c, 256) for c in counts]
            + [rowblock(c, 256) for c in counts]
            + [pl.BlockSpec((None, FLAGS, c), lambda i, *_: (i, 0, 0)) for c in counts]
            + [whole(a.shape) for a in new],
            out_specs=rowblock(block, width),
            scratch_shapes=[pltpu.VMEM((block, width), F32)]
            + [pltpu.VMEM((c, 256), F32) for c in counts]
            + [pltpu.VMEM((c, 256), F32) for c in counts]
            + [pltpu.VMEM((FLAGS, c), F32) for c in counts]
            + [pltpu.VMEM((2, block, 128), F32)] * 3,
        ),
        out_shape=jax.ShapeDtypeStruct((rows, width), BF16),
        compiler_params=params(),
        cost_estimate=cost(2 * rows * width * 1024, 12 * rows * width),
        name="slide_finish",
    )(gid, start, pos, tokens, emb, wso, *qs, *sums, *tops, *new)


def shifted(x, axis, size, by):
    return lax.ppermute(x, axis, [(i, (i + by) % size) for i in range(size)])


def gather_shifts(x, axis, size):
    got = [x]
    for k in range(1, size):
        got.append(shifted(x, axis, size, k))
    return got


def after(x, *others):
    return lax.optimization_barrier((x,) + others)[0]


def gather_line(x, axis, size, place, gate, pick=True):
    if size != 4:
        got = gather_shifts(x, axis, size)
        return got if pick else got[:1] + [(g, g) for g in got[1:]]
    right = lax.ppermute(x, axis, [(0, 1), (1, 2), (2, 3)])
    left = lax.ppermute(x, axis, [(3, 2), (2, 1), (1, 0)])
    ends, pass_right, pass_left = x, right, left
    if gate:
        ends, pass_right, pass_left = lax.optimization_barrier((x, right, left) + tuple(gate))[:3]
    right_two = lax.ppermute(pass_right, axis, [(1, 2), (2, 3)])
    left_two = lax.ppermute(pass_left, axis, [(2, 1), (1, 0)])
    across = lax.ppermute(ends, axis, [(0, 3), (3, 0)])
    pairs = [(right, across), (right_two, left_two), (across, left)]
    if not pick:
        return [x] + pairs
    return [x] + [jnp.where(place >= k, *pair) for k, pair in enumerate(pairs, 1)]


def swapped(x, axis, size, bit):
    return lax.ppermute(x, axis, [(i, i ^ bit) for i in range(size)])


def shards(
    tile_patches,
    w_patch,
    w_tqkv,
    w_to,
    w_gu,
    w_down,
    tile_gain,
    w_in,
    slide_tokens,
    slide_gain,
    w_sqkv,
    w_so,
    pattern_of_group,
    new_positions,
):
    devs = lax.axis_size("dev")
    grps = lax.axis_size("grp")
    dev = lax.axis_index("dev")
    grp = lax.axis_index("grp")
    rows, width = slide_tokens.shape
    place = grp * devs + dev
    ratios = (1, devs, devs * grps // 4, devs * grps)
    counts = [rows // r for r in ratios]
    group_width = width // GROUPS
    news = new_positions.shape[0]

    ring_dev = lax.rem(dev - lax.iota(jnp.int32, devs) + devs, devs)

    patches = gather_shifts(tile_patches, "dev", devs)

    gid = jnp.sum(
        jnp.where(
            pattern_of_group[None, :] == lax.iota(jnp.int32, 4)[:, None], lax.iota(jnp.int32, GROUPS)[None, :], 0
        ),
        axis=1,
    ).astype(jnp.int32)
    gain_row = slide_gain.reshape(1, width)
    q0, q1, q2, q3, kv0, kv_near, kv_far, w_slide = slide_proj(gid, slide_tokens, gain_row, w_sqkv, ratios)
    qs = [q0, q1, q2, q3]

    pieces = grps
    while (w_to.shape[0] // pieces) % 16:
        pieces //= 2
    piece_rows = w_to.shape[0] // pieces
    mine = lax.dynamic_slice_in_dim(w_to, lax.rem(grp, pieces) * piece_rows, piece_rows, 0)
    far_rows = kv_far.shape[0]
    chunks = kv_far.shape[1] // (2 * USED)
    together = pieces == grps and kv_far.shape[1] == w_to.shape[1]
    bits = [1 << b for b in range(grps.bit_length() - 1)]
    bits = bits[1:] + bits[:1]

    def plane(x, count):
        held, tags = [jnp.stack(gather_shifts(x, "dev", devs))], [0]
        for bit in bits:
            if bit < count:
                held = held + [swapped(h, "grp", grps, bit) for h in held]
                tags = tags + [t ^ bit for t in tags]
        return held, tags

    if together:
        far, tags = plane(jnp.concatenate([mine, kv_far], axis=0), grps)
        lasts, sources, last_row = far, tags, piece_rows
    else:
        far, tags = plane(mine, pieces)
        lasts, sources = plane(kv_far, grps)
        last_row = 0
    order = jnp.bitwise_xor(lax.rem(grp, pieces), jnp.array(tags, jnp.int32))
    order = jnp.concatenate([order, dev[None]])

    x0, att = tile_front(ring_dev, patches, w_patch, w_tqkv, tile_gain)
    atts = gather_line(att, "dev", devs, dev, (), pick=False)
    arrived = [a for pair in atts[1:] for a in pair]

    kv_near = after(kv_near, *patches)
    shipped = gather_line(kv_near, "dev", devs, dev, tuple(arrived))
    tails = [jnp.stack([x[counts[1] :] for x in shipped])]
    near_sources = [0]
    near = grps // 4
    for bit in [1 << b for b in range(near.bit_length() - 1)]:
        tails = tails + [swapped(t, "grp", grps, bit) for t in tails]
        near_sources = near_sources + [t ^ bit for t in near_sources]
    kvs = [
        ([kv0], [0], [((0, rows), 0)]),
        (shipped, list(range(devs)), [((0, counts[1]), 0)] * devs),
        (
            tails,
            [t for t in range(len(tails)) for _ in range(devs)],
            [(k, (0, counts[2]), 0) for _ in tails for k in range(devs)],
        ),
        (
            lasts,
            [t for t in range(len(lasts)) for _ in range(devs * chunks)],
            [
                (k, (last_row, last_row + far_rows), c * 2 * USED)
                for _ in lasts
                for k in range(devs)
                for c in range(chunks)
            ],
        ),
    ]

    def devices_of(tags):
        return (jnp.bitwise_xor(grp, jnp.array(tags, jnp.int32))[:, None] * devs + ring_dev[None]).reshape(-1)

    blocks = [place[None], devices_of([0]), devices_of(near_sources), devices_of(sources)]
    at = jnp.stack(
        [
            (blocks[p][:, None] * rows + lax.iota(jnp.int32, counts[p])[None] * ratios[p]).reshape(1, rows)
            for p in range(4)
        ]
    )
    at = after(at, *patches)

    block = slide_block(rows, ratios)
    first_half = slide_attend(new_positions, at[0], after(q0, att), kvs[0], 1, block, 0)
    states = [slide_attend(new_positions, at[0], q0, kvs[0], 1, block, 1, first_half)]
    x0 = after(x0, *states[0])
    for p in range(1, 4):
        states.append(slide_attend(new_positions, at[p], qs[p], kvs[p], ratios[p], block // ratios[p]))
    sums = [a for a, _ in states]
    tops = [b for _, b in states]

    pooled = tile_back(x0, atts, w_to, far, w_gu, w_down, tile_gain, order)
    parts = jnp.stack(gather_shifts(pooled[0], "dev", devs))
    tiles = x0.shape[0] // PATCHES
    tile_embed = embed(ring_dev, parts, pooled[1], tile_gain, w_in, tiles)
    every = [tile_embed]
    tags = [0]
    for bit in bits:
        every = every + [swapped(e, "grp", grps, bit) for e in every]
        tags = tags + [t ^ bit for t in tags]
    every = jnp.concatenate(every, axis=0)
    owners = jnp.bitwise_xor(grp, jnp.array(tags, jnp.int32))
    new_here = new_positions.reshape(grps, tiles)[owners].reshape(news)

    slots = -(-news // 16) * 16
    padded = jnp.pad(every, ((0, slots - news), (0, 0))).astype(F32)
    pos_column = jnp.pad(new_here, (0, slots - news)).reshape(slots, 1)
    seg = jnp.stack([place * rows, jnp.int32(rows)]).astype(jnp.int32)
    new = fresh(seg, gid, new_positions, padded, pos_column, gain_row, w_slide, at, kvs, ratios)
    start = (place * rows).reshape(1).astype(jnp.int32)
    slide_out = finish(
        gid,
        start,
        new_here,
        slide_tokens,
        padded,
        w_so.reshape(GROUPS, group_width, width),
        qs,
        sums,
        tops,
        new,
        ratios,
        news,
    )
    return (tile_embed, slide_out)


def solution(mesh):
    placed = (
        P(("grp", "dev"), None),
        P(),
        P(None, None, "dev"),
        P("dev", None),
        P(None, None, "dev"),
        P("dev", None),
        P(),
        P(),
        P(("grp", "dev"), None),
        P(),
        P(),
        P(),
        P(),
        P(),
    )

    return jax.shard_map(
        shards,
        mesh=mesh,
        in_specs=placed,
        out_specs=(P("grp", None), P(("grp", "dev"), None)),
        check_vma=False,
    )
```

```python
import functools
import math

import jax
import jax.numpy as jnp
from jax import lax
from jax.experimental import pallas as pl
from jax.experimental.pallas import tpu as pltpu
from jax.sharding import PartitionSpec as P


TILE_HEAD = 64
PATCHES = 256
SLIDE_HEAD = 48
GROUPS = 4
MASKED = -1e30
LOG2E = math.log2(math.e)
F32 = jnp.float32
BF16 = jnp.bfloat16


def norm(x, gain):
    center = x - jnp.mean(x, axis=-1, keepdims=True)
    spread = jnp.mean(center * center, axis=-1, keepdims=True)
    return center * lax.rsqrt(spread + 1e-06) * gain


def mm(a, b):
    return jnp.dot(a, b, preferred_element_type=F32)


def mmt(a, b):
    return lax.dot_general(a, b, (((1,), (1,)), ((), ())), preferred_element_type=F32)


def lanes(shape):
    return lax.broadcasted_iota(jnp.int32, shape, len(shape) - 1)


def params(mib=60):
    return pltpu.CompilerParams(vmem_limit_bytes=mib * 1024 * 1024)


def cost(flops, bytes_accessed, trans=0):
    return pl.CostEstimate(flops=int(flops), bytes_accessed=int(bytes_accessed), transcendentals=int(trans))


def whole(shape):
    return pl.BlockSpec(shape, lambda *_: (0,) * len(shape))


def tile_front_kernel(devs, where_ref, *rest):
    patch_refs = rest[:devs]
    wp_ref, wqkv_ref, gain_ref, x0_ref, att_ref, held = rest[devs:]
    step = pl.program_id(0)

    @pl.when(step == 0)
    def _():
        count = patch_refs[0].shape[0]
        for k in range(devs):
            held[pl.ds(pl.multiple_of(where_ref[k] * count, count), count), :] = patch_refs[k][...]

    patch = held[pl.ds(pl.multiple_of(step * PATCHES, PATCHES), PATCHES), :]
    x0 = mm(patch, wp_ref[...]).astype(BF16)
    x0_ref[...] = x0
    h1 = norm(x0.astype(F32), gain_ref[0:1, :]).astype(BF16)
    q = (mm(h1, wqkv_ref[0]) * (TILE_HEAD ** -0.5 * LOG2E)).astype(BF16)
    k = mm(h1, wqkv_ref[1]).astype(BF16)
    v = mm(h1, wqkv_ref[2]).astype(BF16)
    width = 2 * TILE_HEAD
    first = lanes((PATCHES, width)) < TILE_HEAD
    for pair in range(q.shape[1] // width):
        cut = slice(pair * width, (pair + 1) * width)
        qp, kp, vp = q[:, cut], k[:, cut], v[:, cut]
        none = jnp.zeros_like(qp)
        both = []
        for s in (mmt(jnp.where(first, qp, none), kp), mmt(jnp.where(first, none, qp), kp)):
            e = jnp.exp2(s - jnp.max(s, axis=1, keepdims=True))
            total = jnp.sum(e, axis=1, keepdims=True)
            both.append(mm(e.astype(BF16), vp) / total)
        att_ref[:, cut] = jnp.where(first, both[0], both[1]).astype(BF16)


def tile_front(where, patches, w_patch, w_tqkv, gain):
    devs = len(patches)
    count, vec = patches[0].shape
    tokens = devs * count
    width = w_patch.shape[1]
    part = w_tqkv.shape[2]
    return pl.pallas_call(
        functools.partial(tile_front_kernel, devs),
        grid=(tokens // PATCHES,),
        in_specs=[pl.BlockSpec(memory_space=pltpu.SMEM)]
        + [whole((count, vec))] * devs
        + [
            whole(w_patch.shape),
            whole(w_tqkv.shape),
            whole(gain.shape),
        ],
        out_specs=[
            pl.BlockSpec((PATCHES, width), lambda i: (i, 0)),
            pl.BlockSpec((PATCHES, part), lambda i: (i, 0)),
        ],
        out_shape=[
            jax.ShapeDtypeStruct((tokens, width), BF16),
            jax.ShapeDtypeStruct((tokens, part), BF16),
        ],
        scratch_shapes=[pltpu.VMEM((tokens, vec), BF16)],
        compiler_params=params(),
        cost_estimate=cost(2 * tokens * width * (vec + 3 * part), 2 * (width * (vec + 3 * part) + tokens * (vec + width + part))),
        name="tile_front",
    )(where, *patches, w_patch, w_tqkv, gain)


def tile_back_kernel(devs, pieces, x0_ref, *rest):
    att_refs = rest[: 2 * devs - 1]
    rest = rest[2 * devs - 1 :]
    far_refs = rest[:pieces]
    (wto_own, wgu_any, wdown_any, gain_ref, order_ref, out_ref, mean_ref, wto, wgu, wdown, hsum, sems) = rest[pieces:]
    step = pl.program_id(0)
    rows = wto_own.shape[0]
    piece = rows // pieces

    def far(k, b):
        place = pl.multiple_of(order_ref[b] * piece, piece)
        return pltpu.make_async_copy(far_refs[b].at[k, pl.ds(0, piece)], wto.at[k, pl.ds(place, piece)], sems.at[k])

    def own():
        return pltpu.make_async_copy(wto_own, wto.at[0], sems.at[0])

    def gu(i):
        return pltpu.make_async_copy(wgu_any.at[i], wgu.at[i], sems.at[devs + i])

    def down():
        return pltpu.make_async_copy(wdown_any, wdown, sems.at[devs + 2])

    @pl.when(step == 0)
    def _():
        own().start()
        for k in range(1, devs):
            for b in range(pieces):
                far(k, b).start()
        gu(0).start()
        gu(1).start()
        down().start()
        hsum[...] = jnp.zeros_like(hsum)
        mean_ref[...] = jnp.zeros_like(mean_ref)
        own().wait()

    x1 = x0_ref[...].astype(F32) + mm(att_refs[0][...], wto[0])
    for k in range(1, devs):

        @pl.when(step == 0)
        def _(k=k):
            for b in range(pieces):
                far(k, b).wait()

        near = order_ref[pieces] >= k
        att = jnp.where(near, att_refs[2 * k - 1][...], att_refs[2 * k][...])
        x1 = x1 + mm(att, wto[k])
    x1 = x1.astype(BF16).astype(F32)
    h2 = norm(x1, gain_ref[1:2, :]).astype(BF16)

    @pl.when(step == 0)
    def _():
        gu(0).wait()
        gu(1).wait()

    gate = mm(h2, wgu[0])
    up = mm(h2, wgu[1])
    hidden = (gate * (1.0 / (1.0 + jnp.exp(-gate))) * up).astype(BF16).astype(F32)
    mean_ref[pl.ds(step, 1), :] = jnp.mean(x1, axis=0, keepdims=True)
    hsum[pl.ds(step, 1), :] = jnp.mean(hidden, axis=0, keepdims=True)

    @pl.when(step == pl.num_programs(0) - 1)
    def _():
        down().wait()
        high = hsum[...].astype(BF16).astype(F32)
        both = mm(jnp.concatenate([high, hsum[...] - high], axis=0).astype(BF16), wdown[...])
        out_ref[...] = both[0:8] + both[8:16]


def tile_back(x0, atts, wto_own, wto_far, w_gu, w_down, gain, order):
    devs = len(atts)
    atts = atts[:1] + [a for pair in atts[1:] for a in pair]
    pieces = len(wto_far)
    tokens, width = x0.shape
    part = atts[0].shape[1]
    hid = w_gu.shape[2]
    anyspec = pl.BlockSpec(memory_space=pl.ANY)
    return pl.pallas_call(
        functools.partial(tile_back_kernel, devs, pieces),
        grid=(tokens // PATCHES,),
        in_specs=[pl.BlockSpec((PATCHES, width), lambda i: (i, 0))]
        + [pl.BlockSpec((PATCHES, part), lambda i: (i, 0))] * (2 * devs - 1)
        + [anyspec] * (pieces + 3)
        + [whole(gain.shape), pl.BlockSpec(memory_space=pltpu.SMEM)],
        out_specs=[whole((8, width))] * 2,
        out_shape=[jax.ShapeDtypeStruct((8, width), F32)] * 2,
        scratch_shapes=[
            pltpu.VMEM((devs, part, width), BF16),
            pltpu.VMEM(w_gu.shape, BF16),
            pltpu.VMEM(w_down.shape, BF16),
            pltpu.VMEM((8, hid), F32),
            pltpu.SemaphoreType.DMA((devs + 3,)),
        ],
        compiler_params=params(),
        cost_estimate=cost(2 * tokens * width * (width + 2 * hid), 2 * width * (width + 3 * hid) + 4 * tokens * width),
        name="tile_back",
    )(x0, *atts, *wto_far, wto_own, w_gu, w_down, gain, order)


def even_sum(refs, first, stride):
    if stride >= len(refs):
        return refs[first][...]
    return even_sum(refs, first, 2 * stride) + even_sum(refs, first + stride, 2 * stride)


def embed_kernel(tiles, *refs):
    mean_ref, gain_ref, win_ref, out_ref = refs[-4:]
    pooled = mean_ref[...] + even_sum(refs[:-4], 0, 1)
    normed = norm(pooled, gain_ref[2:3, :]).astype(BF16)
    out_ref[...] = mm(normed, win_ref[...])[:tiles].astype(BF16)


def embed(parts, mean, gain, w_in, tiles):
    return pl.pallas_call(
        functools.partial(embed_kernel, tiles),
        in_specs=[pl.BlockSpec(memory_space=pltpu.VMEM)] * (len(parts) + 3),
        out_specs=pl.BlockSpec(memory_space=pltpu.VMEM),
        out_shape=jax.ShapeDtypeStruct((tiles, w_in.shape[1]), BF16),
        compiler_params=params(),
        cost_estimate=cost(16 * w_in.shape[0] * w_in.shape[1], 2 * w_in.shape[0] * w_in.shape[1]),
        name="tile_embed",
    )(*parts, mean, gain, w_in)


USED = GROUPS * SLIDE_HEAD
FLAGS = 256 - USED
SHARE = FLAGS // GROUPS


def group_for(pattern_ref, p):
    group = jnp.int32(0)
    for g in range(1, GROUPS):
        group = group + jnp.where(pattern_ref[g] == p, g, 0)
    return group


def between(lane, low, count):
    return jnp.logical_and(lane >= low, lane < low + count)


def own_q(lane, h):
    return between(lane, FLAGS + SLIDE_HEAD * h, SLIDE_HEAD)


def own_sum(lane, h):
    return jnp.logical_or(between(lane, SLIDE_HEAD * h, SLIDE_HEAD), between(lane, USED + SHARE * h, SHARE))


def flagged(q):
    return jnp.where(lanes(q.shape) < GROUPS, 1.0, q).astype(BF16)


def one_head(q, lane, h):
    return jnp.where(own_q(lane, h), q, jnp.where(lane == h, 1.0, 0.0).astype(q.dtype))


def slide_proj_kernel(ratios, gid_ref, x_ref, gain_ref, w_any, *rest):
    q_refs = rest[0:4]
    kv0_ref, near_ref, far_ref, w_ref, held = rest[4:9]
    block, width = x_ref.shape
    scale = SLIDE_HEAD ** -0.5 * LOG2E
    step = pl.program_id(0)

    @pl.when(step == 0)
    def _():
        w_ref[:, :, 0:FLAGS] = jnp.zeros((GROUPS, width, FLAGS), BF16)
        for g in range(GROUPS):
            cut = slice(g * USED, (g + 1) * USED)
            w_ref[g, :, FLAGS:256] = w_any[0, :, cut]
            w_ref[g, :, 256 : 256 + USED] = w_any[2, :, cut]
            w_ref[g, :, 256 + USED : 256 + 2 * USED] = w_any[1, :, cut]

    hs = norm(x_ref[...].astype(F32), gain_ref[...].reshape(1, -1)).astype(BF16)
    wide = hs.astype(F32)
    for c in range(held.shape[0]):
        held[c] = wide[:, c * 128 : (c + 1) * 128]
    y = mm(hs, w_ref[group_for(gid_ref, 0)])
    q_refs[0][...] = flagged(y[:, :256] * scale)
    kv0_ref[...] = y[:, 256:].astype(BF16)
    base = 0
    for p in range(1, 4):
        ratio = ratios[p]
        count = block // ratio
        rows = jnp.concatenate(
            [
                jnp.concatenate(
                    [held[c, pl.ds(j % ratio, count, stride=ratio), :] for j in range(GROUPS)], axis=0
                )
                for c in range(held.shape[0])
            ],
            axis=1,
        ).astype(BF16)
        y = mm(rows, w_ref[group_for(gid_ref, p)])
        lane = lanes((count, y.shape[1])) - FLAGS
        kept = y[0:count]
        for j in range(1, GROUPS):
            here = between(lane, SLIDE_HEAD * j, SLIDE_HEAD)
            here = jnp.logical_or(here, between(lane, USED + SLIDE_HEAD * j, SLIDE_HEAD))
            here = jnp.logical_or(here, between(lane, 2 * USED + SLIDE_HEAD * j, SLIDE_HEAD))
            kept = jnp.where(here, y[j * count : (j + 1) * count], kept)
        q_refs[p][...] = flagged(kept[:, :256] * scale)
        if p == 3:
            far_ref[...] = kept[:, 256:].astype(BF16)
        else:
            spot = pl.multiple_of(base + step * count, 16)
            near_ref[pl.ds(spot, count), :] = kept[:, 256:].astype(BF16)
            base = base + count * pl.num_programs(0)


def slide_block(rows, ratios):
    return min(rows, 16 * ratios[3])


def finish_block(rows, ratios):
    return min(rows, 2 * slide_block(rows, ratios))


def slide_proj(gid, tokens, gain, w, ratios):
    rows, width = tokens.shape
    block = slide_block(rows, ratios)
    counts = [rows // r for r in ratios]
    wide = (GROUPS, width, 256 + 2 * USED)
    return pl.pallas_call(
        functools.partial(slide_proj_kernel, ratios),
        grid_spec=pltpu.PrefetchScalarGridSpec(
            num_scalar_prefetch=1,
            grid=(rows // block,),
            in_specs=[
                pl.BlockSpec((block, width), lambda i, g: (i, 0)),
                whole(gain.shape),
                whole(w.shape),
            ],
            out_specs=[pl.BlockSpec((block // r, 256), lambda i, g: (i, 0)) for r in ratios]
            + [
                pl.BlockSpec((block, 2 * USED), lambda i, g: (i, 0)),
                whole((sum(counts[1:3]), 2 * USED)),
                pl.BlockSpec((block // ratios[3], 2 * USED), lambda i, g: (0, i)),
                whole(wide),
            ],
            scratch_shapes=[pltpu.VMEM((width // 128, block, 128), F32)],
        ),
        out_shape=[jax.ShapeDtypeStruct((c, 256), BF16) for c in counts]
        + [
            jax.ShapeDtypeStruct((rows, 2 * USED), BF16),
            jax.ShapeDtypeStruct((sum(counts[1:3]), 2 * USED), BF16),
            jax.ShapeDtypeStruct((block // ratios[3], rows // block * 2 * USED), BF16),
            jax.ShapeDtypeStruct(wide, BF16),
        ],
        compiler_params=params(),
        cost_estimate=cost(2 * rows * width * 640 * 2.6, 2 * rows * width * 3 + 2 * w.size),
        name="slide_proj",
    )(gid, tokens, gain, w)


def augment(pieces, at, ratio, pos_ref, news, ka, va):
    keys = ka.shape[0]
    head = lax.broadcasted_iota(jnp.int32, (8, keys), 0)
    here = jnp.broadcast_to(at, (8, keys))
    if ratio > 1:
        here = here + head
    low = jnp.zeros((8, keys), F32)
    for n in range(news):
        low = jnp.where(here == pos_ref[n], MASKED, low)
    spread = jnp.where(lanes((8, 256)) == lax.broadcasted_iota(jnp.int32, (8, 256), 0), 1.0, 0.0).astype(BF16)
    low = lax.dot_general(
        low.astype(BF16), spread, (((0,), (0,)), ((), ())), preferred_element_type=F32
    ).astype(BF16)
    spot = 0
    for load in pieces:
        value, key = load()
        count = value.shape[0]
        lane = lanes((count, 256))
        cut = slice(spot, spot + count)
        ka[cut] = jnp.where(lane < FLAGS, low[cut], key)
        va[cut] = jnp.where(lane < USED, value, jnp.ones_like(value))
        spot += count


def state(sums, tops):
    rows = sums.shape[0]
    low = sums[:, 128:256]
    lane = lanes((rows, 128))
    for h in range(GROUPS):
        low = jnp.where(between(lane, USED - 128 + SHARE * h + 8, 8), tops[h], low)
    return jnp.transpose(low)[USED - 128 :]


def attend(q, ka, va):
    rows = q.shape[0]
    lane = lanes(q.shape)
    tops = []
    sums = jnp.zeros((rows, 256), F32)
    s = mmt(one_head(q, lane, 0), ka[...])
    for h in range(GROUPS):
        after = mmt(one_head(q, lane, h + 1), ka[...]) if h + 1 < GROUPS else None
        m = jnp.max(s, axis=1, keepdims=True)
        o = mm(jnp.exp2(s - m).astype(BF16), va[...])
        sums = jnp.where(own_sum(lane, h), o, sums)
        tops.append(m)
        s = after
    return sums, state(sums, tops)


def attend_stacked(q, ka, va):
    rows = q.shape[0]
    lane = lanes(q.shape)
    s = mmt(jnp.concatenate([one_head(q, lane, h) for h in range(GROUPS)], axis=0), ka[...])
    m = jnp.max(s, axis=1, keepdims=True)
    o = mm(jnp.exp2(s - m).astype(BF16), va[...])
    sums = o[0:rows]
    for h in range(1, GROUPS):
        sums = jnp.where(own_sum(lane, h), o[h * rows : (h + 1) * rows], sums)
    return sums, state(sums, [m[h * rows : (h + 1) * rows] for h in range(GROUPS)])


def loaders(refs, cuts):
    made = []
    for ref, cut in zip(refs, cuts):

        def load(ref=ref, cut=cut):
            index = cut[:-2] + (slice(cut[-2][0], cut[-2][1]),)
            lane = cut[-1]
            return ref[index + (slice(lane, lane + 256),)], ref[index + (slice(lane + 128, lane + 384),)]

        made.append(load)
    return made


def slide_attend_kernel(ratio, news, cuts, used, pos_ref, at_ref, q_ref, *rest):
    count = max(used) + 1
    kv_refs = rest[:count]
    sum_ref, top_ref, ka, va = rest[-4:]

    @pl.when(pl.program_id(0) == 0)
    def _():
        augment(loaders([kv_refs[u] for u in used], cuts), at_ref[...], ratio, pos_ref, news, ka, va)

    small = q_ref.shape[0] < 128
    sums, tops = (attend_stacked if small else attend)(q_ref[...], ka, va)
    sum_ref[...] = sums
    if len(top_ref.shape) == 2:
        top_ref[...] = tops
    else:
        size = top_ref.shape[2]
        for u in range(top_ref.shape[0]):
            top_ref[u] = tops[:, u * size : (u + 1) * size]


def slide_attend(pos, at, q, kv, ratio, size, half=None, earlier=()):
    arrays, used, cuts = kv
    rows = q.shape[0]
    keys = at.shape[1]
    block = min(rows, 256)
    steps = rows // block
    first = 0
    if half is not None:
        first, steps = half * (steps // 2), steps // 2
    smem = pl.BlockSpec(memory_space=pltpu.SMEM)
    if block <= size:
        per = size // block
        top_spec = pl.BlockSpec((None, FLAGS, block), lambda i: ((i + first) // per, 0, (i + first) % per))
    else:
        top_spec = pl.BlockSpec((block // size, FLAGS, size), lambda i: (i + first, 0, 0))
    done = steps * block
    return pl.pallas_call(
        functools.partial(slide_attend_kernel, ratio, pos.shape[0], cuts, used),
        grid=(steps,),
        in_specs=[
            smem,
            whole(at.shape),
            pl.BlockSpec((block, 256), lambda i: (i + first, 0)),
        ]
        + [whole(a.shape) for a in arrays]
        + [pl.BlockSpec(memory_space=pl.ANY)] * len(earlier),
        out_specs=[
            pl.BlockSpec((block, 256), lambda i: (i + first, 0)),
            top_spec,
        ]
        + ([] if half == 0 else [whole((keys, 256))] * 2),
        out_shape=[
            jax.ShapeDtypeStruct((rows, 256), F32),
            jax.ShapeDtypeStruct((rows // size, FLAGS, size), F32),
        ]
        + ([] if half == 0 else [jax.ShapeDtypeStruct((keys, 256), BF16)] * 2),
        scratch_shapes=[pltpu.VMEM((keys, 256), BF16), pltpu.VMEM((keys, 256), BF16)] if half == 0 else [],
        input_output_aliases={3 + len(arrays) + i: i for i in range(len(earlier))},
        compiler_params=params(),
        cost_estimate=cost(4 * 4 * done * keys * 256, 2 * keys * 384 + 6 * done * 256, 4 * done * keys),
    )(pos, at, q, *arrays, *earlier)


def fresh_kernel(ratios, news, seg_ref, gid_ref, emb_ref, pos_ref, gain_ref, w_ref, *rest):
    far_refs = rest[:8]
    q_ref, sum_ref, top_ref, ka_ref, va_ref, held, queries, sems = rest[8:]

    def fetch(i):
        return pltpu.make_async_copy(far_refs[i], held.at[i], sems.at[i])

    for i in range(8):
        fetch(i).start()
    scale = SLIDE_HEAD ** -0.5 * LOG2E
    hs = norm(emb_ref[...], gain_ref[...].reshape(1, -1)).astype(BF16)
    slots = emb_ref.shape[0]
    pos = pos_ref[...]
    lane = lanes((slots, 256))
    row = lax.broadcasted_iota(jnp.int32, (slots, 256), 0)
    for p in range(4):
        y = mm(hs, w_ref[group_for(gid_ref, p)])
        q = flagged(y[:, :256] * scale)
        kv = y[:, 256:].astype(BF16)
        span = ratios[p] * seg_ref[1]
        same = (pos // span) == (seg_ref[0] // span)
        seen = jnp.broadcast_to(same, lane.shape)
        if ratios[p] > 1:
            seen = jnp.logical_and(seen, lax.rem(pos, ratios[p]) == lane)
        seen = jnp.logical_and(seen, row < news)
        flag = jnp.where(seen, 0.0, MASKED).astype(BF16)
        none = jnp.zeros_like(flag)
        for h in range(GROUPS):
            key = jnp.where(own_q(lane, h), kv[:, 128:384], jnp.where(lane == h, flag, none))
            ka_ref[p, h * slots : (h + 1) * slots] = key
            va_ref[p, h * slots : (h + 1) * slots] = jnp.where(between(lane, SLIDE_HEAD * h, SLIDE_HEAD), kv[:, 0:256], none)
        q_ref[p] = q.astype(F32)
        queries[p] = q

    def pattern(p, carry):
        for i in range(2):
            spot = 2 * p + i
            pltpu.make_async_copy(far_refs[0], held.at[spot], sems.at[spot]).wait()
        sums, tops = attend_stacked(queries[p], held.at[2 * p], held.at[2 * p + 1])
        sum_ref[p] = sums
        top_ref[p] = tops
        return carry

    lax.fori_loop(0, 4, pattern, 0)


def fresh(seg, gid, emb, pos, gain, w, augmented, ratios, news):
    slots = emb.shape[0]
    keys = augmented[0].shape[0]
    smem = pl.BlockSpec(memory_space=pltpu.SMEM)
    vmem = pl.BlockSpec(memory_space=pltpu.VMEM)
    return pl.pallas_call(
        functools.partial(fresh_kernel, ratios, news),
        in_specs=[smem] * 2 + [vmem] * 4 + [pl.BlockSpec(memory_space=pl.ANY)] * 8,
        out_specs=[vmem] * 5,
        out_shape=[
            jax.ShapeDtypeStruct((4, slots, 256), F32),
            jax.ShapeDtypeStruct((4, slots, 256), F32),
            jax.ShapeDtypeStruct((4, FLAGS, slots), F32),
            jax.ShapeDtypeStruct((4, GROUPS * slots, 256), BF16),
            jax.ShapeDtypeStruct((4, GROUPS * slots, 256), BF16),
        ],
        scratch_shapes=[
            pltpu.VMEM((8, keys, 256), BF16),
            pltpu.VMEM((4, slots, 256), BF16),
            pltpu.SemaphoreType.DMA((8,)),
        ],
        compiler_params=params(),
        cost_estimate=cost(4 * 4 * 4 * slots * keys * 256, 2 * w.size + 16 * keys * 256, 16 * slots * keys),
        name="slide_fresh",
    )(seg, gid, emb, pos, gain, w, *augmented)


def finish_kernel(ratios, news, gid_ref, start_ref, pos_ref, x_ref, emb_ref, wso_ref, *rest):
    q_refs = rest[0:4]
    sum_refs = rest[4:8]
    top_refs = rest[8:12]
    nq_ref, nsum_ref, ntop_ref, nka_ref, nva_ref, out_ref = rest[12:18]
    seq = rest[18]
    qs = rest[19:23]
    ss = rest[23:27]
    ts = rest[27:31]
    placed = rest[31:34]
    step = pl.program_id(0)
    block = x_ref.shape[0]
    start = start_ref[0] + step * block
    seq[...] = x_ref[...].astype(F32)
    for p in range(4):
        qs[p][...] = q_refs[p][...].astype(F32)
        ss[p][...] = sum_refs[p][...]
        ts[p][...] = top_refs[p][...]

    @pl.when(step == 0)
    def _():
        for p in range(1, 4):
            placed[p - 1][...] = jnp.zeros_like(placed[p - 1])

    lane = lanes((1, 256))

    def patch(n, carry):
        row = pos_ref[n] - start

        @pl.when(jnp.logical_and(row >= 0, row < block))
        def _():
            one = pl.ds(n, 1)
            seq[pl.ds(row, 1), :] = emb_ref[one, :]
            for p in range(4):
                spot = row // ratios[p]
                at = pl.ds(spot, 1)
                fresh_state = ntop_ref[p]
                column = jnp.sum(jnp.where(lanes(fresh_state.shape) == n, fresh_state, 0.0), axis=1, keepdims=True)
                held_state = ts[p][...]
                mine = lanes(held_state.shape) == spot
                if ratios[p] == 1:
                    qs[p][at, :] = nq_ref[p, one, :]
                    ss[p][at, :] = nsum_ref[p, one, :]
                else:
                    head = lax.rem(pos_ref[n], ratios[p])
                    fits = head < GROUPS
                    mine_q = jnp.logical_and(own_q(lane, head), fits)
                    mine_sum = jnp.logical_and(own_sum(lane, head), fits)
                    qs[p][at, :] = jnp.where(mine_q, nq_ref[p, one, :], qs[p][at, :])
                    ss[p][at, :] = jnp.where(mine_sum, nsum_ref[p, one, :], ss[p][at, :])
                    line = lax.broadcasted_iota(jnp.int32, held_state.shape, 0)
                    mine = jnp.logical_and(mine, between(line, SHARE * head, SHARE))
                ts[p][...] = jnp.where(mine, column, held_state)

        return carry

    lax.fori_loop(0, news, patch, 0)

    slots = nka_ref.shape[1] // GROUPS
    owner = lanes((24, 256)) // SLIDE_HEAD
    spread = jnp.where(owner == lax.rem(lax.broadcasted_iota(jnp.int32, (24, 256), 0), 8), 1.0, 0.0).astype(BF16)
    scores = [mmt(nka_ref[p], qs[p][...].astype(BF16)) for p in range(4)]
    weights, splits = [], []
    for p in range(4):
        count = block // ratios[p]
        scale = jnp.zeros((8, count), F32)
        line = lax.broadcasted_iota(jnp.int32, (8, count), 0)
        parts = []
        for h in range(GROUPS):
            own = scores[p][h * slots : (h + 1) * slots]
            total = ts[p][SHARE * h : SHARE * h + 1]
            old = ts[p][SHARE * h + 8 : SHARE * h + 9]
            top = jnp.maximum(old, jnp.max(own, axis=0, keepdims=True))
            e = jnp.exp2(own - top)
            shrink = jnp.exp2(old - top)
            inverse = 1.0 / (total * shrink + jnp.sum(e, axis=0, keepdims=True))
            parts.append((e * inverse).astype(BF16))
            scale = jnp.where(line == h, shrink * inverse, scale)
        weights.append(jnp.concatenate(parts, axis=0))
        high = scale.astype(BF16).astype(F32)
        middle = (scale - high).astype(BF16).astype(F32)
        splits.append(jnp.concatenate([high, middle, scale - high - middle], axis=0).astype(BF16))
    first = (((0,), (0,)), ((), ()))
    outs = [
        lax.dot_general(weights[p], nva_ref[p], first, preferred_element_type=F32) for p in range(4)
    ]
    wides = [lax.dot_general(splits[p], spread, first, preferred_element_type=F32) for p in range(4)]
    values = [ss[p][...] * wides[p] + outs[p] for p in range(4)]
    for p in range(1, 4):
        count = block // ratios[p]
        lane_wide = lanes((count, 256))
        for j in range(GROUPS):
            own = jnp.where(between(lane_wide, SLIDE_HEAD * j, SLIDE_HEAD), values[p], 0.0)
            for c in range(2):
                at = pl.ds(j, count, stride=ratios[p])
                placed[p - 1][c, at, :] = own[:, c * 128 : (c + 1) * 128]
    atts = [values[0][:, :USED].astype(BF16)] + [
        jnp.concatenate([placed[p - 1][0], placed[p - 1][1]], axis=1)[:, :USED].astype(BF16) for p in range(1, 4)
    ]
    result = seq[...]
    for p in range(4):
        result = result + mm(atts[p], wso_ref[group_for(gid_ref, p)])
    out_ref[...] = result.astype(BF16)


def finish(gid, start, pos, tokens, emb, wso, qs, sums, tops, new, ratios, news):
    rows, width = tokens.shape
    block = finish_block(rows, ratios)
    counts = [block // r for r in ratios]

    def rowblock(n, lanes_here):
        return pl.BlockSpec((n, lanes_here), lambda i, *_: (i, 0))

    return pl.pallas_call(
        functools.partial(finish_kernel, ratios, news),
        grid_spec=pltpu.PrefetchScalarGridSpec(
            num_scalar_prefetch=3,
            grid=(rows // block,),
            in_specs=[rowblock(block, width), whole(emb.shape), whole(wso.shape)]
            + [rowblock(c, 256) for c in counts]
            + [rowblock(c, 256) for c in counts]
            + [pl.BlockSpec((None, FLAGS, c), lambda i, *_: (i, 0, 0)) for c in counts]
            + [whole(a.shape) for a in new],
            out_specs=rowblock(block, width),
            scratch_shapes=[pltpu.VMEM((block, width), F32)]
            + [pltpu.VMEM((c, 256), F32) for c in counts]
            + [pltpu.VMEM((c, 256), F32) for c in counts]
            + [pltpu.VMEM((FLAGS, c), F32) for c in counts]
            + [pltpu.VMEM((2, block, 128), F32)] * 3,
        ),
        out_shape=jax.ShapeDtypeStruct((rows, width), BF16),
        compiler_params=params(),
        cost_estimate=cost(2 * rows * width * 1024, 12 * rows * width),
        name="slide_finish",
    )(gid, start, pos, tokens, emb, wso, *qs, *sums, *tops, *new)


def shifted(x, axis, size, by):
    return lax.ppermute(x, axis, [(i, (i + by) % size) for i in range(size)])


def gather_shifts(x, axis, size):
    got = [x]
    for k in range(1, size):
        got.append(shifted(x, axis, size, k))
    return got


def after(x, *others):
    return lax.optimization_barrier((x,) + others)[0]


def gather_line(x, axis, size, place, gate, pick=True):
    if size != 4:
        got = gather_shifts(x, axis, size)
        return got if pick else got[:1] + [(g, g) for g in got[1:]]
    right = lax.ppermute(x, axis, [(0, 1), (1, 2), (2, 3)])
    left = lax.ppermute(x, axis, [(3, 2), (2, 1), (1, 0)])
    ends, pass_right, pass_left = x, right, left
    if gate:
        ends, pass_right, pass_left = lax.optimization_barrier((x, right, left) + tuple(gate))[:3]
    right_two = lax.ppermute(pass_right, axis, [(1, 2), (2, 3)])
    left_two = lax.ppermute(pass_left, axis, [(2, 1), (1, 0)])
    across = lax.ppermute(ends, axis, [(0, 3), (3, 0)])
    pairs = [(right, across), (right_two, left_two), (across, left)]
    if not pick:
        return [x] + pairs
    return [x] + [jnp.where(place >= k, *pair) for k, pair in enumerate(pairs, 1)]


def swapped(x, axis, size, bit):
    return lax.ppermute(x, axis, [(i, i ^ bit) for i in range(size)])


def shards(
    tile_patches,
    w_patch,
    w_tqkv,
    w_to,
    w_gu,
    w_down,
    tile_gain,
    w_in,
    slide_tokens,
    slide_gain,
    w_sqkv,
    w_so,
    pattern_of_group,
    new_positions,
):
    devs = lax.axis_size("dev")
    grps = lax.axis_size("grp")
    dev = lax.axis_index("dev")
    grp = lax.axis_index("grp")
    rows, width = slide_tokens.shape
    place = grp * devs + dev
    ratios = (1, devs, devs * grps // 4, devs * grps)
    counts = [rows // r for r in ratios]
    group_width = width // GROUPS
    news = new_positions.shape[0]

    ring_dev = lax.rem(dev - lax.iota(jnp.int32, devs) + devs, devs)

    patches = gather_shifts(tile_patches, "dev", devs)

    gid = pattern_of_group
    gain_row = slide_gain
    q0, q1, q2, q3, kv0, kv_near, kv_far, w_slide = slide_proj(gid, slide_tokens, gain_row, w_sqkv, ratios)
    qs = [q0, q1, q2, q3]

    pieces = grps
    while (w_to.shape[0] // pieces) % 16:
        pieces //= 2
    piece_rows = w_to.shape[0] // pieces
    mine = lax.dynamic_slice_in_dim(w_to, lax.rem(grp, pieces) * piece_rows, piece_rows, 0)
    far_rows = kv_far.shape[0]
    chunks = kv_far.shape[1] // (2 * USED)
    together = pieces == grps and kv_far.shape[1] == w_to.shape[1]
    bits = [1 << b for b in range(grps.bit_length() - 1)]
    bits = bits[1:] + bits[:1]

    def plane(x, count):
        held, tags = [jnp.stack(gather_shifts(x, "dev", devs))], [0]
        for bit in bits:
            if bit < count:
                held = held + [swapped(h, "grp", grps, bit) for h in held]
                tags = tags + [t ^ bit for t in tags]
        return held, tags

    if together:
        far, tags = plane(jnp.concatenate([mine, kv_far], axis=0), grps)
        lasts, sources, last_row = far, tags, piece_rows
    else:
        far, tags = plane(mine, pieces)
        lasts, sources = plane(kv_far, grps)
        last_row = 0
    order = jnp.bitwise_xor(lax.rem(grp, pieces), jnp.array(tags, jnp.int32))
    order = jnp.concatenate([order, dev[None]])

    x0, att = tile_front(ring_dev, patches, w_patch, w_tqkv, tile_gain)
    atts = gather_line(att, "dev", devs, dev, (), pick=False)
    arrived = [a for pair in atts[1:] for a in pair]

    kv_near = after(kv_near, *patches)
    shipped = gather_line(kv_near, "dev", devs, dev, tuple(arrived))
    tails = [jnp.stack([x[counts[1] :] for x in shipped])]
    near_sources = [0]
    near = grps // 4
    for bit in [1 << b for b in range(near.bit_length() - 1)]:
        tails = tails + [swapped(t, "grp", grps, bit) for t in tails]
        near_sources = near_sources + [t ^ bit for t in near_sources]
    kvs = [
        ([kv0], [0], [((0, rows), 0)]),
        (shipped, list(range(devs)), [((0, counts[1]), 0)] * devs),
        (
            tails,
            [t for t in range(len(tails)) for _ in range(devs)],
            [(k, (0, counts[2]), 0) for _ in tails for k in range(devs)],
        ),
        (
            lasts,
            [t for t in range(len(lasts)) for _ in range(devs * chunks)],
            [
                (k, (last_row, last_row + far_rows), c * 2 * USED)
                for _ in lasts
                for k in range(devs)
                for c in range(chunks)
            ],
        ),
    ]

    def devices_of(tags):
        return (jnp.bitwise_xor(grp, jnp.array(tags, jnp.int32))[:, None] * devs + ring_dev[None]).reshape(-1)

    blocks = [place[None], devices_of([0]), devices_of(near_sources), devices_of(sources)]
    at = jnp.stack(
        [
            (blocks[p][:, None] * rows + lax.iota(jnp.int32, counts[p])[None] * ratios[p]).reshape(1, rows)
            for p in range(4)
        ]
    )
    at = after(at, *patches)

    block = finish_block(rows, ratios)
    first_half = slide_attend(new_positions, at[0], after(q0, att), kvs[0], 1, block, 0)
    states = [slide_attend(new_positions, at[0], q0, kvs[0], 1, block, 1, first_half)]
    x0 = after(x0, states[0][0])
    for p in range(1, 4):
        states.append(slide_attend(new_positions, at[p], qs[p], kvs[p], ratios[p], block // ratios[p]))
    sums = [state[0] for state in states]
    tops = [state[1] for state in states]

    part, mean = tile_back(x0, atts, w_to, far, w_gu, w_down, tile_gain, order)
    parts = gather_shifts(part, "dev", devs)
    tiles = x0.shape[0] // PATCHES
    tile_embed = embed(parts, mean, tile_gain, w_in, tiles)
    every = [tile_embed]
    tags = [0]
    for bit in bits:
        every = every + [swapped(e, "grp", grps, bit) for e in every]
        tags = tags + [t ^ bit for t in tags]
    every = jnp.concatenate(every, axis=0)
    owners = jnp.bitwise_xor(grp, jnp.array(tags, jnp.int32))
    new_here = new_positions.reshape(grps, tiles)[owners].reshape(news)

    slots = -(-news // 16) * 16
    padded = jnp.pad(every, ((0, slots - news), (0, 0))).astype(F32)
    pos_column = jnp.pad(new_here, (0, slots - news)).reshape(slots, 1)
    seg = jnp.stack([place * rows, jnp.int32(rows)]).astype(jnp.int32)
    augmented = [a for state in states for a in state[2:]]
    new = fresh(seg, gid, padded, pos_column, gain_row, w_slide, augmented, ratios, news)
    start = (place * rows).reshape(1).astype(jnp.int32)
    slide_out = finish(
        gid,
        start,
        new_here,
        slide_tokens,
        padded,
        w_so.reshape(GROUPS, group_width, width),
        qs,
        sums,
        tops,
        new,
        ratios,
        news,
    )
    return (tile_embed, slide_out)


def solution(mesh):
    placed = (
        P(("grp", "dev"), None),
        P(),
        P(None, None, "dev"),
        P("dev", None),
        P(None, None, "dev"),
        P("dev", None),
        P(),
        P(),
        P(("grp", "dev"), None),
        P(),
        P(),
        P(),
        P(),
        P(),
    )

    return jax.shard_map(
        shards,
        mesh=mesh,
        in_specs=placed,
        out_specs=(P("grp", None), P(("grp", "dev"), None)),
        check_vma=False,
    )
```

```python
import functools
import math

import jax
import jax.numpy as jnp
from jax import lax
from jax.experimental import pallas as pl
from jax.experimental.pallas import tpu as pltpu
from jax.sharding import PartitionSpec as P


TILE_HEAD = 64
PATCHES = 256
SLIDE_HEAD = 48
GROUPS = 4
MASKED = -1e30
LOG2E = math.log2(math.e)
F32 = jnp.float32
BF16 = jnp.bfloat16


def norm(x, gain):
    center = x - jnp.mean(x, axis=-1, keepdims=True)
    spread = jnp.mean(center * center, axis=-1, keepdims=True)
    return center * lax.rsqrt(spread + 1e-06) * gain


def mm(a, b):
    return jnp.dot(a, b, preferred_element_type=F32)


def mmt(a, b):
    return lax.dot_general(a, b, (((1,), (1,)), ((), ())), preferred_element_type=F32)


def lanes(shape):
    return lax.broadcasted_iota(jnp.int32, shape, len(shape) - 1)


def params(mib=60):
    return pltpu.CompilerParams(vmem_limit_bytes=mib * 1024 * 1024)


def cost(flops, bytes_accessed, trans=0):
    return pl.CostEstimate(flops=int(flops), bytes_accessed=int(bytes_accessed), transcendentals=int(trans))


def whole(shape):
    return pl.BlockSpec(shape, lambda *_: (0,) * len(shape))


def tile_front_kernel(devs, where_ref, *rest):
    patch_refs = rest[:devs]
    wp_ref, wqkv_ref, gain_ref, x0_ref, att_ref, held = rest[devs:]
    step = pl.program_id(0)

    @pl.when(step == 0)
    def _():
        count = patch_refs[0].shape[0]
        for k in range(devs):
            held[pl.ds(pl.multiple_of(where_ref[k] * count, count), count), :] = patch_refs[k][...]

    patch = held[pl.ds(pl.multiple_of(step * PATCHES, PATCHES), PATCHES), :]
    x0 = mm(patch, wp_ref[...]).astype(BF16)
    x0_ref[...] = x0
    h1 = norm(x0.astype(F32), gain_ref[0:1, :]).astype(BF16)
    q = (mm(h1, wqkv_ref[0]) * (TILE_HEAD ** -0.5 * LOG2E)).astype(BF16)
    k = mm(h1, wqkv_ref[1]).astype(BF16)
    v = mm(h1, wqkv_ref[2]).astype(BF16)
    width = 2 * TILE_HEAD
    first = lanes((PATCHES, width)) < TILE_HEAD
    for pair in range(q.shape[1] // width):
        cut = slice(pair * width, (pair + 1) * width)
        qp, kp, vp = q[:, cut], k[:, cut], v[:, cut]
        none = jnp.zeros_like(qp)
        both = []
        for s in (mmt(jnp.where(first, qp, none), kp), mmt(jnp.where(first, none, qp), kp)):
            e = jnp.exp2(s - jnp.max(s, axis=1, keepdims=True))
            total = jnp.sum(e, axis=1, keepdims=True)
            both.append(mm(e.astype(BF16), vp) * (1.0 / total))
        att_ref[:, cut] = jnp.where(first, both[0], both[1]).astype(BF16)


def tile_front(where, patches, w_patch, w_tqkv, gain):
    devs = len(patches)
    count, vec = patches[0].shape
    tokens = devs * count
    width = w_patch.shape[1]
    part = w_tqkv.shape[2]
    return pl.pallas_call(
        functools.partial(tile_front_kernel, devs),
        grid=(tokens // PATCHES,),
        in_specs=[pl.BlockSpec(memory_space=pltpu.SMEM)]
        + [whole((count, vec))] * devs
        + [
            whole(w_patch.shape),
            whole(w_tqkv.shape),
            whole(gain.shape),
        ],
        out_specs=[
            pl.BlockSpec((PATCHES, width), lambda i: (i, 0)),
            pl.BlockSpec((PATCHES, part), lambda i: (i, 0)),
        ],
        out_shape=[
            jax.ShapeDtypeStruct((tokens, width), BF16),
            jax.ShapeDtypeStruct((tokens, part), BF16),
        ],
        scratch_shapes=[pltpu.VMEM((tokens, vec), BF16)],
        compiler_params=params(),
        cost_estimate=cost(2 * tokens * width * (vec + 3 * part), 2 * (width * (vec + 3 * part) + tokens * (vec + width + part))),
        name="tile_front",
    )(where, *patches, w_patch, w_tqkv, gain)


def tile_back_kernel(devs, pieces, x0_ref, *rest):
    att_refs = rest[: 2 * devs - 1]
    rest = rest[2 * devs - 1 :]
    far_refs = rest[:pieces]
    (wto_own, wgu_any, wdown_any, gain_ref, order_ref, out_ref, mean_ref, wto, wgu, wdown, hsum, sems) = rest[pieces:]
    step = pl.program_id(0)
    rows = wto_own.shape[0]
    piece = rows // pieces

    def far(k, b):
        place = pl.multiple_of(order_ref[b] * piece, piece)
        return pltpu.make_async_copy(far_refs[b].at[k, pl.ds(0, piece)], wto.at[k, pl.ds(place, piece)], sems.at[k])

    def own():
        return pltpu.make_async_copy(wto_own, wto.at[0], sems.at[0])

    def gu(i):
        return pltpu.make_async_copy(wgu_any.at[i], wgu.at[i], sems.at[devs + i])

    def down():
        return pltpu.make_async_copy(wdown_any, wdown, sems.at[devs + 2])

    @pl.when(step == 0)
    def _():
        own().start()
        for k in range(1, devs):
            for b in range(pieces):
                far(k, b).start()
        gu(0).start()
        gu(1).start()
        down().start()
        hsum[...] = jnp.zeros_like(hsum)
        mean_ref[...] = jnp.zeros_like(mean_ref)
        own().wait()

    x1 = x0_ref[...].astype(F32) + mm(att_refs[0][...], wto[0])
    for k in range(1, devs):

        @pl.when(step == 0)
        def _(k=k):
            for b in range(pieces):
                far(k, b).wait()

        near = order_ref[pieces] >= k
        att = jnp.where(near, att_refs[2 * k - 1][...], att_refs[2 * k][...])
        x1 = x1 + mm(att, wto[k])
    x1 = x1.astype(BF16).astype(F32)
    h2 = norm(x1, gain_ref[1:2, :]).astype(BF16)

    @pl.when(step == 0)
    def _():
        gu(0).wait()
        gu(1).wait()

    gate = mm(h2, wgu[0])
    up = mm(h2, wgu[1])
    hidden = (gate * (1.0 / (1.0 + jnp.exp(-gate))) * up).astype(BF16).astype(F32)
    mean_ref[pl.ds(step, 1), :] = jnp.mean(x1, axis=0, keepdims=True)
    hsum[pl.ds(step, 1), :] = jnp.mean(hidden, axis=0, keepdims=True)

    @pl.when(step == pl.num_programs(0) - 1)
    def _():
        down().wait()
        high = hsum[...].astype(BF16).astype(F32)
        both = mm(jnp.concatenate([high, hsum[...] - high], axis=0).astype(BF16), wdown[...])
        out_ref[...] = both[0:8] + both[8:16]


def tile_back(x0, atts, wto_own, wto_far, w_gu, w_down, gain, order):
    devs = len(atts)
    atts = atts[:1] + [a for pair in atts[1:] for a in pair]
    pieces = len(wto_far)
    tokens, width = x0.shape
    part = atts[0].shape[1]
    hid = w_gu.shape[2]
    anyspec = pl.BlockSpec(memory_space=pl.ANY)
    return pl.pallas_call(
        functools.partial(tile_back_kernel, devs, pieces),
        grid=(tokens // PATCHES,),
        in_specs=[pl.BlockSpec((PATCHES, width), lambda i: (i, 0))]
        + [pl.BlockSpec((PATCHES, part), lambda i: (i, 0))] * (2 * devs - 1)
        + [anyspec] * (pieces + 3)
        + [whole(gain.shape), pl.BlockSpec(memory_space=pltpu.SMEM)],
        out_specs=[whole((8, width))] * 2,
        out_shape=[jax.ShapeDtypeStruct((8, width), F32)] * 2,
        scratch_shapes=[
            pltpu.VMEM((devs, part, width), BF16),
            pltpu.VMEM(w_gu.shape, BF16),
            pltpu.VMEM(w_down.shape, BF16),
            pltpu.VMEM((8, hid), F32),
            pltpu.SemaphoreType.DMA((devs + 3,)),
        ],
        compiler_params=params(),
        cost_estimate=cost(2 * tokens * width * (width + 2 * hid), 2 * width * (width + 3 * hid) + 4 * tokens * width),
        name="tile_back",
    )(x0, *atts, *wto_far, wto_own, w_gu, w_down, gain, order)


def even_sum(refs, first, stride):
    if stride >= len(refs):
        return refs[first][...]
    return even_sum(refs, first, 2 * stride) + even_sum(refs, first + stride, 2 * stride)


def embed_kernel(tiles, *refs):
    mean_ref, gain_ref, win_ref, out_ref = refs[-4:]
    pooled = mean_ref[...] + even_sum(refs[:-4], 0, 1)
    normed = norm(pooled, gain_ref[2:3, :]).astype(BF16)
    out_ref[...] = mm(normed, win_ref[...])[:tiles].astype(BF16)


def embed(parts, mean, gain, w_in, tiles):
    return pl.pallas_call(
        functools.partial(embed_kernel, tiles),
        in_specs=[pl.BlockSpec(memory_space=pltpu.VMEM)] * (len(parts) + 3),
        out_specs=pl.BlockSpec(memory_space=pltpu.VMEM),
        out_shape=jax.ShapeDtypeStruct((tiles, w_in.shape[1]), BF16),
        compiler_params=params(),
        cost_estimate=cost(16 * w_in.shape[0] * w_in.shape[1], 2 * w_in.shape[0] * w_in.shape[1]),
        name="tile_embed",
    )(*parts, mean, gain, w_in)


USED = GROUPS * SLIDE_HEAD
FLAGS = 256 - USED
SHARE = FLAGS // GROUPS


def group_for(pattern_ref, p):
    group = jnp.int32(0)
    for g in range(1, GROUPS):
        group = group + jnp.where(pattern_ref[g] == p, g, 0)
    return group


def between(lane, low, count):
    return jnp.logical_and(lane >= low, lane < low + count)


def own_q(lane, h):
    return between(lane, FLAGS + SLIDE_HEAD * h, SLIDE_HEAD)


def own_sum(lane, h):
    return jnp.logical_or(between(lane, SLIDE_HEAD * h, SLIDE_HEAD), between(lane, USED + SHARE * h, SHARE))


def flagged(q):
    return jnp.where(lanes(q.shape) < GROUPS, 1.0, q).astype(BF16)


def one_head(q, lane, h):
    return jnp.where(own_q(lane, h), q, jnp.where(lane == h, 1.0, 0.0).astype(q.dtype))


def slide_proj_kernel(ratios, gid_ref, x_ref, gain_ref, w_any, *rest):
    q_refs = rest[0:4]
    kv0_ref, near_ref, far_ref, w_ref, held = rest[4:9]
    block, width = x_ref.shape
    scale = SLIDE_HEAD ** -0.5 * LOG2E
    step = pl.program_id(0)

    @pl.when(step == 0)
    def _():
        w_ref[:, :, 0:FLAGS] = jnp.zeros((GROUPS, width, FLAGS), BF16)
        for g in range(GROUPS):
            cut = slice(g * USED, (g + 1) * USED)
            w_ref[g, :, FLAGS:256] = w_any[0, :, cut]
            w_ref[g, :, 256 : 256 + USED] = w_any[2, :, cut]
            w_ref[g, :, 256 + USED : 256 + 2 * USED] = w_any[1, :, cut]

    hs = norm(x_ref[...].astype(F32), gain_ref[...].reshape(1, -1)).astype(BF16)
    wide = hs.astype(F32)
    for c in range(held.shape[0]):
        held[c] = wide[:, c * 128 : (c + 1) * 128]
    y = mm(hs, w_ref[group_for(gid_ref, 0)])
    q_refs[0][...] = flagged(y[:, :256] * scale)
    kv0_ref[...] = y[:, 256:].astype(BF16)
    base = 0
    for p in range(1, 4):
        ratio = ratios[p]
        count = block // ratio
        rows = jnp.concatenate(
            [
                jnp.concatenate(
                    [held[c, pl.ds(j % ratio, count, stride=ratio), :] for j in range(GROUPS)], axis=0
                )
                for c in range(held.shape[0])
            ],
            axis=1,
        ).astype(BF16)
        y = mm(rows, w_ref[group_for(gid_ref, p)])
        lane = lanes((count, y.shape[1])) - FLAGS
        kept = y[0:count]
        for j in range(1, GROUPS):
            here = between(lane, SLIDE_HEAD * j, SLIDE_HEAD)
            here = jnp.logical_or(here, between(lane, USED + SLIDE_HEAD * j, SLIDE_HEAD))
            here = jnp.logical_or(here, between(lane, 2 * USED + SLIDE_HEAD * j, SLIDE_HEAD))
            kept = jnp.where(here, y[j * count : (j + 1) * count], kept)
        q_refs[p][...] = flagged(kept[:, :256] * scale)
        if p == 3:
            far_ref[...] = kept[:, 256:].astype(BF16)
        else:
            spot = pl.multiple_of(base + step * count, 16)
            near_ref[pl.ds(spot, count), :] = kept[:, 256:].astype(BF16)
            base = base + count * pl.num_programs(0)


def slide_block(rows, ratios):
    return min(rows, 16 * ratios[3])


def finish_block(rows, ratios):
    return min(rows, 2 * slide_block(rows, ratios))


def slide_proj(gid, tokens, gain, w, ratios):
    rows, width = tokens.shape
    block = slide_block(rows, ratios)
    counts = [rows // r for r in ratios]
    wide = (GROUPS, width, 256 + 2 * USED)
    return pl.pallas_call(
        functools.partial(slide_proj_kernel, ratios),
        grid_spec=pltpu.PrefetchScalarGridSpec(
            num_scalar_prefetch=1,
            grid=(rows // block,),
            in_specs=[
                pl.BlockSpec((block, width), lambda i, g: (i, 0)),
                whole(gain.shape),
                whole(w.shape),
            ],
            out_specs=[pl.BlockSpec((block // r, 256), lambda i, g: (i, 0)) for r in ratios]
            + [
                pl.BlockSpec((block, 2 * USED), lambda i, g: (i, 0)),
                whole((sum(counts[1:3]), 2 * USED)),
                pl.BlockSpec((block // ratios[3], 2 * USED), lambda i, g: (0, i)),
                whole(wide),
            ],
            scratch_shapes=[pltpu.VMEM((width // 128, block, 128), F32)],
        ),
        out_shape=[jax.ShapeDtypeStruct((c, 256), BF16) for c in counts]
        + [
            jax.ShapeDtypeStruct((rows, 2 * USED), BF16),
            jax.ShapeDtypeStruct((sum(counts[1:3]), 2 * USED), BF16),
            jax.ShapeDtypeStruct((block // ratios[3], rows // block * 2 * USED), BF16),
            jax.ShapeDtypeStruct(wide, BF16),
        ],
        compiler_params=params(),
        cost_estimate=cost(2 * rows * width * 640 * 2.6, 2 * rows * width * 3 + 2 * w.size),
        name="slide_proj",
    )(gid, tokens, gain, w)


def augment(pieces, at, ratio, pos_ref, news, ka, va):
    keys = ka.shape[0]
    head = lax.broadcasted_iota(jnp.int32, (8, keys), 0)
    here = jnp.broadcast_to(at, (8, keys))
    if ratio > 1:
        here = here + head
    low = jnp.zeros((8, keys), F32)
    for n in range(news):
        low = jnp.where(here == pos_ref[n], MASKED, low)
    spread = jnp.where(lanes((8, 256)) == lax.broadcasted_iota(jnp.int32, (8, 256), 0), 1.0, 0.0).astype(BF16)
    low = lax.dot_general(
        low.astype(BF16), spread, (((0,), (0,)), ((), ())), preferred_element_type=F32
    ).astype(BF16)
    spot = 0
    for load in pieces:
        value, key = load()
        count = value.shape[0]
        lane = lanes((count, 256))
        cut = slice(spot, spot + count)
        ka[cut] = jnp.where(lane < FLAGS, low[cut], key)
        va[cut] = jnp.where(lane < USED, value, jnp.ones_like(value))
        spot += count


def state(sums, tops):
    rows = sums.shape[0]
    low = sums[:, 128:256]
    lane = lanes((rows, 128))
    for h in range(GROUPS):
        low = jnp.where(between(lane, USED - 128 + SHARE * h + 8, 8), tops[h], low)
    return jnp.transpose(low)[USED - 128 :]


def attend(q, ka, va):
    rows = q.shape[0]
    lane = lanes(q.shape)
    tops = []
    sums = jnp.zeros((rows, 256), F32)
    s = mmt(one_head(q, lane, 0), ka[...])
    for h in range(GROUPS):
        after = mmt(one_head(q, lane, h + 1), ka[...]) if h + 1 < GROUPS else None
        m = jnp.max(s, axis=1, keepdims=True)
        o = mm(jnp.exp2(s - m).astype(BF16), va[...])
        sums = jnp.where(own_sum(lane, h), o, sums)
        tops.append(m)
        s = after
    return sums, state(sums, tops)


def attend_stacked(q, ka, va):
    rows = q.shape[0]
    lane = lanes(q.shape)
    s = mmt(jnp.concatenate([one_head(q, lane, h) for h in range(GROUPS)], axis=0), ka[...])
    m = jnp.max(s, axis=1, keepdims=True)
    o = mm(jnp.exp2(s - m).astype(BF16), va[...])
    sums = o[0:rows]
    for h in range(1, GROUPS):
        sums = jnp.where(own_sum(lane, h), o[h * rows : (h + 1) * rows], sums)
    return sums, state(sums, [m[h * rows : (h + 1) * rows] for h in range(GROUPS)])


def loaders(refs, used, cuts, dev_ref):
    made = []
    for use, cut in zip(used, cuts):

        def part(ref, cut):
            index = cut[:-2] + (slice(cut[-2][0], cut[-2][1]),)
            lane = cut[-1]
            return ref[index + (slice(lane, lane + 256),)], ref[index + (slice(lane + 128, lane + 384),)]

        def load(use=use, cut=cut, part=part):
            if isinstance(use, int):
                return part(refs[use], cut)
            near = dev_ref[0] >= use[2]
            first, second = part(refs[use[0]], cut), part(refs[use[1]], cut)
            return tuple(jnp.where(near, a, b) for a, b in zip(first, second))

        made.append(load)
    return made


def slide_attend_kernel(ratio, news, cuts, used, count, dev_ref, pos_ref, at_ref, q_ref, *rest):
    kv_refs = rest[:count]
    sum_ref, top_ref, ka, va = rest[-4:]

    @pl.when(pl.program_id(0) == 0)
    def _():
        augment(loaders(kv_refs, used, cuts, dev_ref), at_ref[...], ratio, pos_ref, news, ka, va)

    small = q_ref.shape[0] < 128
    sums, tops = (attend_stacked if small else attend)(q_ref[...], ka, va)
    sum_ref[...] = sums
    if len(top_ref.shape) == 2:
        top_ref[...] = tops
    else:
        size = top_ref.shape[2]
        for u in range(top_ref.shape[0]):
            top_ref[u] = tops[:, u * size : (u + 1) * size]


def slide_attend(dev, pos, at, q, kv, ratio, size, half=None, earlier=()):
    arrays, used, cuts, views = kv
    rows = q.shape[0]
    keys = at.shape[1]
    block = min(rows, 256)
    steps = rows // block
    first = 0
    if half is not None:
        first, steps = half * (steps // 2), steps // 2
    smem = pl.BlockSpec(memory_space=pltpu.SMEM)
    if block <= size:
        per = size // block
        top_spec = pl.BlockSpec((None, FLAGS, block), lambda i: ((i + first) // per, 0, (i + first) % per))
    else:
        top_spec = pl.BlockSpec((block // size, FLAGS, size), lambda i: (i + first, 0, 0))
    done = steps * block
    return pl.pallas_call(
        functools.partial(slide_attend_kernel, ratio, pos.shape[0], cuts, used, len(arrays)),
        grid=(steps,),
        in_specs=[
            smem,
            smem,
            whole(at.shape),
            pl.BlockSpec((block, 256), lambda i: (i + first, 0)),
        ]
        + [pl.BlockSpec(shape, lambda i, spot=spot: spot) for shape, spot in views]
        + [pl.BlockSpec(memory_space=pl.ANY)] * len(earlier),
        out_specs=[
            pl.BlockSpec((block, 256), lambda i: (i + first, 0)),
            top_spec,
        ]
        + ([] if half == 0 else [whole((keys, 256))] * 2),
        out_shape=[
            jax.ShapeDtypeStruct((rows, 256), F32),
            jax.ShapeDtypeStruct((rows // size, FLAGS, size), F32),
        ]
        + ([] if half == 0 else [jax.ShapeDtypeStruct((keys, 256), BF16)] * 2),
        scratch_shapes=[pltpu.VMEM((keys, 256), BF16), pltpu.VMEM((keys, 256), BF16)] if half == 0 else [],
        input_output_aliases={4 + len(arrays) + i: i for i in range(len(earlier))},
        compiler_params=params(),
        cost_estimate=cost(4 * 4 * done * keys * 256, 2 * keys * 384 + 6 * done * 256, 4 * done * keys),
    )(dev, pos, at, q, *arrays, *earlier)


def new_spot(pos_ref, grp, n, tiles, bits):
    index = n // tiles
    tag = 0
    for b, bit in enumerate(bits):
        tag = tag + (index // (1 << b)) % 2 * bit
    return pos_ref[jnp.bitwise_xor(grp, tag) * tiles + n % tiles]


def fresh_kernel(ratios, rows, bits, place_ref, gid_ref, news_ref, gain_ref, w_ref, *rest):
    far_refs = rest[:8]
    pieces = rest[8 : 8 + (1 << len(bits))]
    emb_ref, q_ref, sum_ref, top_ref, ka_ref, va_ref, held, queries, sems = rest[8 + len(pieces) :]

    def fetch(i):
        return pltpu.make_async_copy(far_refs[i], held.at[i], sems.at[i])

    for i in range(8):
        fetch(i).start()
    scale = SLIDE_HEAD ** -0.5 * LOG2E
    slots = emb_ref.shape[0]
    tiles = pieces[0].shape[0]
    news = len(pieces) * tiles
    emb_ref[...] = jnp.zeros_like(emb_ref)
    for i, piece in enumerate(pieces):
        emb_ref[i * tiles : (i + 1) * tiles, :] = piece[...].astype(F32)
    hs = norm(emb_ref[...], gain_ref[...].reshape(1, -1)).astype(BF16)
    pos = jnp.zeros((slots, 1), jnp.int32)
    line = lax.broadcasted_iota(jnp.int32, (slots, 1), 0)
    for n in range(news):
        pos = jnp.where(line == n, new_spot(news_ref, place_ref[1], n, tiles, bits), pos)
    lane = lanes((slots, 256))
    row = lax.broadcasted_iota(jnp.int32, (slots, 256), 0)
    for p in range(4):
        y = mm(hs, w_ref[group_for(gid_ref, p)])
        q = flagged(y[:, :256] * scale)
        kv = y[:, 256:].astype(BF16)
        span = ratios[p] * rows
        same = (pos // span) == (place_ref[0] // span)
        seen = jnp.broadcast_to(same, lane.shape)
        if ratios[p] > 1:
            seen = jnp.logical_and(seen, lax.rem(pos, ratios[p]) == lane)
        seen = jnp.logical_and(seen, row < news)
        flag = jnp.where(seen, 0.0, MASKED).astype(BF16)
        none = jnp.zeros_like(flag)
        for h in range(GROUPS):
            key = jnp.where(own_q(lane, h), kv[:, 128:384], jnp.where(lane == h, flag, none))
            ka_ref[p, h * slots : (h + 1) * slots] = key
            va_ref[p, h * slots : (h + 1) * slots] = jnp.where(between(lane, SLIDE_HEAD * h, SLIDE_HEAD), kv[:, 0:256], none)
        q_ref[p] = q.astype(F32)
        queries[p] = q

    def pattern(p, carry):
        for i in range(2):
            spot = 2 * p + i
            pltpu.make_async_copy(far_refs[0], held.at[spot], sems.at[spot]).wait()
        sums, tops = attend_stacked(queries[p], held.at[2 * p], held.at[2 * p + 1])
        sum_ref[p] = sums
        top_ref[p] = tops
        return carry

    lax.fori_loop(0, 4, pattern, 0)


def fresh(place, gid, news_pos, gain, w, augmented, pieces, ratios, rows, bits):
    news = news_pos.shape[0]
    slots = -(-news // 16) * 16
    keys = augmented[0].shape[0]
    width = w.shape[1]
    smem = pl.BlockSpec(memory_space=pltpu.SMEM)
    vmem = pl.BlockSpec(memory_space=pltpu.VMEM)
    return pl.pallas_call(
        functools.partial(fresh_kernel, ratios, rows, bits),
        in_specs=[smem] * 3 + [vmem] * 2 + [pl.BlockSpec(memory_space=pl.ANY)] * 8 + [vmem] * len(pieces),
        out_specs=[vmem] * 6,
        out_shape=[
            jax.ShapeDtypeStruct((slots, width), F32),
            jax.ShapeDtypeStruct((4, slots, 256), F32),
            jax.ShapeDtypeStruct((4, slots, 256), F32),
            jax.ShapeDtypeStruct((4, FLAGS, slots), F32),
            jax.ShapeDtypeStruct((4, GROUPS * slots, 256), BF16),
            jax.ShapeDtypeStruct((4, GROUPS * slots, 256), BF16),
        ],
        scratch_shapes=[
            pltpu.VMEM((8, keys, 256), BF16),
            pltpu.VMEM((4, slots, 256), BF16),
            pltpu.SemaphoreType.DMA((8,)),
        ],
        compiler_params=params(),
        cost_estimate=cost(4 * 4 * 4 * slots * keys * 256, 2 * w.size + 16 * keys * 256, 16 * slots * keys),
        name="slide_fresh",
    )(place, gid, news_pos, gain, w, *augmented, *pieces)


def finish_kernel(ratios, news, tiles, bits, gid_ref, start_ref, pos_ref, x_ref, emb_ref, wso_ref, *rest):
    q_refs = rest[0:4]
    sum_refs = rest[4:8]
    top_refs = rest[8:12]
    nq_ref, nsum_ref, ntop_ref, nka_ref, nva_ref, out_ref = rest[12:18]
    seq = rest[18]
    qs = rest[19:23]
    ss = rest[23:27]
    ts = rest[27:31]
    placed = rest[31:34]
    spots = rest[34]
    step = pl.program_id(0)
    block = x_ref.shape[0]
    start = start_ref[0] + step * block
    seq[...] = x_ref[...].astype(F32)
    for p in range(4):
        qs[p][...] = q_refs[p][...].astype(F32)
        ss[p][...] = sum_refs[p][...]
        ts[p][...] = top_refs[p][...]

    @pl.when(step == 0)
    def _():
        for p in range(1, 4):
            placed[p - 1][...] = jnp.zeros_like(placed[p - 1])

    lane = lanes((1, 256))

    @pl.when(step == 0)
    def _():
        for n in range(news):
            spots[n] = new_spot(pos_ref, start_ref[1], n, tiles, bits)

    def patch(n, carry):
        spot_here = spots[n]
        row = spot_here - start

        @pl.when(jnp.logical_and(row >= 0, row < block))
        def _():
            one = pl.ds(n, 1)
            seq[pl.ds(row, 1), :] = emb_ref[one, :]
            for p in range(4):
                spot = row // ratios[p]
                at = pl.ds(spot, 1)
                fresh_state = ntop_ref[p]
                column = jnp.sum(jnp.where(lanes(fresh_state.shape) == n, fresh_state, 0.0), axis=1, keepdims=True)
                held_state = ts[p][...]
                mine = lanes(held_state.shape) == spot
                if ratios[p] == 1:
                    qs[p][at, :] = nq_ref[p, one, :]
                    ss[p][at, :] = nsum_ref[p, one, :]
                else:
                    head = lax.rem(spot_here, ratios[p])
                    fits = head < GROUPS
                    mine_q = jnp.logical_and(own_q(lane, head), fits)
                    mine_sum = jnp.logical_and(own_sum(lane, head), fits)
                    qs[p][at, :] = jnp.where(mine_q, nq_ref[p, one, :], qs[p][at, :])
                    ss[p][at, :] = jnp.where(mine_sum, nsum_ref[p, one, :], ss[p][at, :])
                    line = lax.broadcasted_iota(jnp.int32, held_state.shape, 0)
                    mine = jnp.logical_and(mine, between(line, SHARE * head, SHARE))
                ts[p][...] = jnp.where(mine, column, held_state)

        return carry

    lax.fori_loop(0, news, patch, 0)

    slots = nka_ref.shape[1] // GROUPS
    owner = lanes((24, 256)) // SLIDE_HEAD
    spread = jnp.where(owner == lax.rem(lax.broadcasted_iota(jnp.int32, (24, 256), 0), 8), 1.0, 0.0).astype(BF16)
    scores = [mmt(nka_ref[p], qs[p][...].astype(BF16)) for p in range(4)]
    weights, splits = [], []
    for p in range(4):
        count = block // ratios[p]
        scale = jnp.zeros((8, count), F32)
        line = lax.broadcasted_iota(jnp.int32, (8, count), 0)
        parts = []
        for h in range(GROUPS):
            own = scores[p][h * slots : (h + 1) * slots]
            total = ts[p][SHARE * h : SHARE * h + 1]
            old = ts[p][SHARE * h + 8 : SHARE * h + 9]
            top = jnp.maximum(old, jnp.max(own, axis=0, keepdims=True))
            e = jnp.exp2(own - top)
            shrink = jnp.exp2(old - top)
            inverse = 1.0 / (total * shrink + jnp.sum(e, axis=0, keepdims=True))
            parts.append((e * inverse).astype(BF16))
            scale = jnp.where(line == h, shrink * inverse, scale)
        weights.append(jnp.concatenate(parts, axis=0))
        high = scale.astype(BF16).astype(F32)
        middle = (scale - high).astype(BF16).astype(F32)
        splits.append(jnp.concatenate([high, middle, scale - high - middle], axis=0).astype(BF16))
    first = (((0,), (0,)), ((), ()))
    outs = [
        lax.dot_general(weights[p], nva_ref[p], first, preferred_element_type=F32) for p in range(4)
    ]
    wides = [lax.dot_general(splits[p], spread, first, preferred_element_type=F32) for p in range(4)]
    values = [ss[p][...] * wides[p] + outs[p] for p in range(4)]
    for p in range(1, 4):
        count = block // ratios[p]
        lane_wide = lanes((count, 256))
        for j in range(GROUPS):
            own = jnp.where(between(lane_wide, SLIDE_HEAD * j, SLIDE_HEAD), values[p], 0.0)
            for c in range(2):
                at = pl.ds(j, count, stride=ratios[p])
                placed[p - 1][c, at, :] = own[:, c * 128 : (c + 1) * 128]
    atts = [values[0][:, :USED].astype(BF16)] + [
        jnp.concatenate([placed[p - 1][0], placed[p - 1][1]], axis=1)[:, :USED].astype(BF16) for p in range(1, 4)
    ]
    result = seq[...]
    for p in range(4):
        result = result + mm(atts[p], wso_ref[group_for(gid_ref, p)])
    out_ref[...] = result.astype(BF16)


def finish(gid, start, pos, tokens, emb, wso, qs, sums, tops, new, ratios, tiles, bits):
    news = pos.shape[0]
    rows, width = tokens.shape
    block = finish_block(rows, ratios)
    counts = [block // r for r in ratios]

    def rowblock(n, lanes_here):
        return pl.BlockSpec((n, lanes_here), lambda i, *_: (i, 0))

    return pl.pallas_call(
        functools.partial(finish_kernel, ratios, news, tiles, bits),
        grid_spec=pltpu.PrefetchScalarGridSpec(
            num_scalar_prefetch=3,
            grid=(rows // block,),
            in_specs=[rowblock(block, width), whole(emb.shape), whole(wso.shape)]
            + [rowblock(c, 256) for c in counts]
            + [rowblock(c, 256) for c in counts]
            + [pl.BlockSpec((None, FLAGS, c), lambda i, *_: (i, 0, 0)) for c in counts]
            + [whole(a.shape) for a in new],
            out_specs=rowblock(block, width),
            scratch_shapes=[pltpu.VMEM((block, width), F32)]
            + [pltpu.VMEM((c, 256), F32) for c in counts]
            + [pltpu.VMEM((c, 256), F32) for c in counts]
            + [pltpu.VMEM((FLAGS, c), F32) for c in counts]
            + [pltpu.VMEM((2, block, 128), F32)] * 3
            + [pltpu.SMEM((news,), jnp.int32)],
        ),
        out_shape=jax.ShapeDtypeStruct((rows, width), BF16),
        compiler_params=params(),
        cost_estimate=cost(2 * rows * width * 1024, 12 * rows * width),
        name="slide_finish",
    )(gid, start, pos, tokens, emb, wso, *qs, *sums, *tops, *new)


def shifted(x, axis, size, by):
    return lax.ppermute(x, axis, [(i, (i + by) % size) for i in range(size)])


def gather_shifts(x, axis, size):
    got = [x]
    for k in range(1, size):
        got.append(shifted(x, axis, size, k))
    return got


def after(x, *others):
    return lax.optimization_barrier((x,) + others)[0]


def gather_line(x, axis, size, place, gate, pick=True):
    if size != 4:
        got = gather_shifts(x, axis, size)
        return got if pick else got[:1] + [(g, g) for g in got[1:]]
    right = lax.ppermute(x, axis, [(0, 1), (1, 2), (2, 3)])
    left = lax.ppermute(x, axis, [(3, 2), (2, 1), (1, 0)])
    ends, pass_right, pass_left = x, right, left
    if gate:
        ends, pass_right, pass_left = lax.optimization_barrier((x, right, left) + tuple(gate))[:3]
    right_two = lax.ppermute(pass_right, axis, [(1, 2), (2, 3)])
    left_two = lax.ppermute(pass_left, axis, [(2, 1), (1, 0)])
    across = lax.ppermute(ends, axis, [(0, 3), (3, 0)])
    pairs = [(right, across), (right_two, left_two), (across, left)]
    if not pick:
        return [x] + pairs
    return [x] + [jnp.where(place >= k, *pair) for k, pair in enumerate(pairs, 1)]


def swapped(x, axis, size, bit):
    return lax.ppermute(x, axis, [(i, i ^ bit) for i in range(size)])


def shards(
    tile_patches,
    w_patch,
    w_tqkv,
    w_to,
    w_gu,
    w_down,
    tile_gain,
    w_in,
    slide_tokens,
    slide_gain,
    w_sqkv,
    w_so,
    pattern_of_group,
    new_positions,
):
    devs = lax.axis_size("dev")
    grps = lax.axis_size("grp")
    dev = lax.axis_index("dev")
    grp = lax.axis_index("grp")
    rows, width = slide_tokens.shape
    place = grp * devs + dev
    ratios = (1, devs, devs * grps // 4, devs * grps)
    counts = [rows // r for r in ratios]
    group_width = width // GROUPS

    ring_dev = lax.rem(dev - lax.iota(jnp.int32, devs) + devs, devs)

    patches = gather_shifts(tile_patches, "dev", devs)

    gid = pattern_of_group
    gain_row = slide_gain
    q0, q1, q2, q3, kv0, kv_near, kv_far, w_slide = slide_proj(gid, slide_tokens, gain_row, w_sqkv, ratios)
    qs = [q0, q1, q2, q3]

    pieces = grps
    while (w_to.shape[0] // pieces) % 16:
        pieces //= 2
    piece_rows = w_to.shape[0] // pieces
    mine = lax.dynamic_slice_in_dim(w_to, lax.rem(grp, pieces) * piece_rows, piece_rows, 0)
    far_rows = kv_far.shape[0]
    chunks = kv_far.shape[1] // (2 * USED)
    together = pieces == grps and piece_rows % far_rows == 0 and kv_far.shape[1] == w_to.shape[1]
    bits = [1 << b for b in range(grps.bit_length() - 1)]
    bits = bits[1:] + bits[:1]

    def plane(x, count):
        held, tags = [jnp.stack(gather_shifts(x, "dev", devs))], [0]
        for bit in bits:
            if bit < count:
                held = held + [swapped(h, "grp", grps, bit) for h in held]
                tags = tags + [t ^ bit for t in tags]
        return held, tags

    if together:
        far, tags = plane(jnp.concatenate([mine, kv_far], axis=0), grps)
        lasts, sources, last_row = far, tags, piece_rows
    else:
        far, tags = plane(mine, pieces)
        lasts, sources = plane(kv_far, grps)
        last_row = 0
    order = jnp.bitwise_xor(lax.rem(grp, pieces), jnp.array(tags, jnp.int32))
    order = jnp.concatenate([order, dev[None]])

    x0, att = tile_front(ring_dev, patches, w_patch, w_tqkv, tile_gain)
    atts = gather_line(att, "dev", devs, dev, (), pick=False)
    arrived = [a for pair in atts[1:] for a in pair]

    shipped = gather_line(kv_near, "dev", devs, dev, tuple(arrived), pick=False)
    dev_here = dev[None]
    arrays, used = [shipped[0]], [0]
    for k, pair in enumerate(shipped[1:], 1):
        spots = []
        for a in pair:
            seen = [i for i, b in enumerate(arrays) if b is a]
            if not seen:
                arrays.append(a)
            spots.append(seen[0] if seen else len(arrays) - 1)
        used.append((spots[0], spots[1], k))
    tails = [
        jnp.stack(
            [shipped[0][counts[1] :]]
            + [jnp.where(dev >= k, a[counts[1] :], b[counts[1] :]) for k, (a, b) in enumerate(shipped[1:], 1)]
        )
    ]
    near_sources = [0]
    near = grps // 4
    for bit in [1 << b for b in range(near.bit_length() - 1)]:
        tails = tails + [swapped(t, "grp", grps, bit) for t in tails]
        near_sources = near_sources + [t ^ bit for t in near_sources]
    kvs = [
        ([kv0], [0], [((0, rows), 0)], [(kv0.shape, (0, 0))]),
        (
            arrays,
            used,
            [((0, counts[1]), 0)] * devs,
            [((counts[1], 2 * USED), (0, 0))] * len(arrays),
        ),
        (
            tails,
            [t for t in range(len(tails)) for _ in range(devs)],
            [(k, (0, counts[2]), 0) for _ in tails for k in range(devs)],
            [(t.shape, (0, 0, 0)) for t in tails],
        ),
        (
            lasts,
            [t for t in range(len(lasts)) for _ in range(devs * chunks)],
            [
                (k, (0, far_rows), c * 2 * USED)
                for _ in lasts
                for k in range(devs)
                for c in range(chunks)
            ],
            [((devs, far_rows, chunks * 2 * USED), (0, last_row // far_rows, 0))] * len(lasts),
        ),
    ]

    def devices_of(tags):
        return (jnp.bitwise_xor(grp, jnp.array(tags, jnp.int32))[:, None] * devs + ring_dev[None]).reshape(-1)

    blocks = [place[None], devices_of([0]), devices_of(near_sources), devices_of(sources)]
    at = jnp.stack(
        [
            (blocks[p][:, None] * rows + lax.iota(jnp.int32, counts[p])[None] * ratios[p]).reshape(1, rows)
            for p in range(4)
        ]
    )
    at = after(at, *patches)

    block = finish_block(rows, ratios)
    first_half = slide_attend(dev_here, new_positions, at[0], after(q0, att), kvs[0], 1, block, 0)
    states = [slide_attend(dev_here, new_positions, at[0], q0, kvs[0], 1, block, 1, first_half)]
    x0 = after(x0, states[0][0])
    for p in range(1, 4):
        states.append(slide_attend(dev_here, new_positions, at[p], qs[p], kvs[p], ratios[p], block // ratios[p]))
    sums = [state[0] for state in states]
    tops = [state[1] for state in states]

    part, mean = tile_back(x0, atts, w_to, far, w_gu, w_down, tile_gain, order)
    parts = gather_shifts(part, "dev", devs)
    tiles = x0.shape[0] // PATCHES
    tile_embed = embed(parts, mean, tile_gain, w_in, tiles)
    every = [tile_embed]
    for bit in bits:
        every = every + [swapped(e, "grp", grps, bit) for e in every]

    here = jnp.stack([place * rows, grp]).astype(jnp.int32)
    emb, *new = fresh(
        here, gid, new_positions, gain_row, w_slide, [a for state in states for a in state[2:]], every, ratios, rows, bits
    )
    slide_out = finish(
        gid,
        here,
        new_positions,
        slide_tokens,
        emb,
        w_so.reshape(GROUPS, group_width, width),
        qs,
        sums,
        tops,
        new,
        ratios,
        tiles,
        bits,
    )
    return (tile_embed, slide_out)


def solution(mesh):
    placed = (
        P(("grp", "dev"), None),
        P(),
        P(None, None, "dev"),
        P("dev", None),
        P(None, None, "dev"),
        P("dev", None),
        P(),
        P(),
        P(("grp", "dev"), None),
        P(),
        P(),
        P(),
        P(),
        P(),
    )

    return jax.shard_map(
        shards,
        mesh=mesh,
        in_specs=placed,
        out_specs=(P("grp", None), P(("grp", "dev"), None)),
        check_vma=False,
    )
```
